128 devices in a mesh: section: 16 (over x, y_lo, core), dp: 4 (over z), tensor: 2 (over y_hi).
Axes of the slice: x: 4, y: 4 (y_hi: 2, y_lo: 2; y = y_hi * 2 + y_lo), z: 4, core: 2. Of those that a mesh axis runs over, the one named last changes fastest.
Arguments:
- block_inputs: bfloat16 [16, 512, 3072], P('section', ('dp', 'tensor')), may hold values from -16 to 16
- qkv_weights: bfloat16 [16, 3, 3072, 3072], P('section', None, None, ('dp', 'tensor')), may hold values from -0.109375 to 0.109375
- out_weights: bfloat16 [16, 3072, 3072], P('section', ('dp', 'tensor')), may hold values from -0.109375 to 0.109375
- norm_gain: float32 [16, 3072], P('section'), may hold values from 0.25 to 1.75
- query_key_gain: float32 [16, 2, 128], P('section'), may hold values from 1.5 to 1.75
- pool_gain: float32 [16, 3072], P('section'), may hold values from 0.25 to 1.75
- class_head: bfloat16 [16, 3072, 512], P('section'), may hold values from -0.75 to 0.75
- labels: int32 [16, 2], P('section'), may hold values from 0 to 511
Outputs:
- out_rows: bfloat16 [16, 512, 3072], P('section', ('dp', 'tensor'))
- query_key_value_gradient: bfloat16 [16, 3, 3072, 3072], P('section', None, None, ('dp', 'tensor'))
- grad_out: bfloat16 [16, 3072, 3072], P('section', ('dp', 'tensor'))
- grad_head: bfloat16 [16, 3072, 512], P('section', ('dp', 'tensor'))
- losses: float32 [16, 2], P('section')
The draws below stay inside these ranges and needn't reach their ends.
All inputs are finite; a program needn't handle non-finite values.
Results may differ from the reference program's by a relative error of at most 0.03.
Values may be sent and summed in bfloat16 or wider, within the bound.
A program may use at most 128 MiB of HBM per device.

```python
import math
import jax
import jax.numpy as jnp
from jax import lax

D = 3072
HEADS = 24
HS = 128
CLASSES = 512
PATCHES = 256
IMAGES = 2
SECTIONS = 16
N_DP = 4
N_TENSOR = 2


def draw_block_inputs(key, part):
    key_columns = jax.random.fold_in(key, 11)
    key_values = jax.random.fold_in(key, 12)
    key_rows = jax.random.fold_in(key, 13)
    full_shape = (SECTIONS, IMAGES * PATCHES, D)
    columns = jnp.exp(jax.random.uniform(key_columns, (SECTIONS, 1, D), minval=math.log(0.3), maxval=math.log(3.0)))
    row_scales = jnp.exp(jax.random.uniform(key_rows, (SECTIONS, IMAGES * PATCHES, 1), minval=math.log(0.25), maxval=math.log(2.0)))
    values = jax.random.normal(key_values, full_shape) * row_scales * columns
    return jnp.clip(values, -16.0, 16.0).astype(jnp.bfloat16)


def touch_ends(entries, rng, low, largest):
    dims = entries.shape
    place = [jax.random.randint(jax.random.fold_in(rng, axis), (), 0, dims[axis]) for axis in range(len(dims))]
    entries = entries.at[tuple(place)].set(low)
    longest = dims.index(max(dims))
    place[longest] = (place[longest] + 1) % dims[longest]
    return entries.at[tuple(place)].set(largest)


def level_of(key, dims, shards, smallest, high):
    factor_of, own = 1.0, jax.random.fold_in(key, 6)
    for dim, shards_of in shards:
        draws = jnp.exp(jax.random.uniform(jax.random.fold_in(own, dim), (shards_of,), jnp.float32, smallest / len(shards), high / len(shards)))
        factor_of = factor_of * jnp.repeat(draws, dims[dim] // shards_of).reshape([-1 if axis == dim else 1 for axis in range(len(dims))])
    return factor_of


def normal_values(rng, shape, scale, limit, pieces=(), held_as=jnp.bfloat16):
    entries = jax.random.normal(rng, shape, jnp.float32) * scale
    if len(pieces) > 0:
        entries = level_of(rng, shape, pieces, -0.22, 0.18) * entries
    return jnp.clip(entries, min=-limit, max=limit).astype(held_as)


def setup_inputs(seed: int = 0) -> dict:
    key_list = jax.random.split(jax.random.key(seed), 9)
    block_inputs = draw_block_inputs(jax.random.fold_in(key_list[8], 71), 0)
    qkv_weights = normal_values(key_list[1], (SECTIONS, 3, D, HEADS * HS), D ** -0.5, 0.109375, ((0, 16), (3, 8)))
    out_weights = normal_values(key_list[2], (SECTIONS, HEADS * HS, D), (HEADS * HS) ** -0.5, 0.109375, ((0, 16), (1, 8)))
    norm_gain = jnp.clip(1.0 + 0.15 * jax.random.normal(key_list[3], (SECTIONS, D), jnp.float32), 0.25, 1.75)
    query_key_gain = jnp.clip(1.5 + 0.25 * jax.random.uniform(key_list[4], (SECTIONS, 2, HS), jnp.float32) ** level_of(key_list[4], (SECTIONS, 2, HS), ((0, 16),), -0.2, 0.2), 1.5, 1.75)
    pool_gain = jnp.clip(1.0 + 0.15 * jax.random.normal(key_list[5], (SECTIONS, D), jnp.float32), 0.25, 1.75)
    class_head = normal_values(key_list[6], (SECTIONS, D, CLASSES), 0.054, 0.75, ((0, 16),))
    labels = touch_ends(jax.random.randint(key_list[7], (SECTIONS, IMAGES), 0, CLASSES), jax.random.fold_in(key_list[7], 1), 0, CLASSES - 1).astype(jnp.int32)
    return {"block_inputs": block_inputs, "qkv_weights": qkv_weights, "out_weights": out_weights, "norm_gain": norm_gain, "query_key_gain": query_key_gain, "pool_gain": pool_gain, "class_head": class_head, "labels": labels}


epsilon = 1e-06

def as_half(values):
    return lax.optimization_barrier(values.astype(jnp.bfloat16))

def into_lone_copy(values):
    return values.astype(jnp.float32)

def norm_last(values, gain_row):
    centered = values - lax.optimization_barrier(jnp.mean(values, axis=-1, keepdims=True))
    inverse = lax.rsqrt(lax.optimization_barrier(jnp.mean(centered * centered, axis=-1, keepdims=True)) + epsilon)
    unit_rows = centered * inverse
    return (unit_rows * gain_row, unit_rows, inverse)

def norm_back(grad_normed, unit_rows, inverse, gain_row):
    scaled = grad_normed * gain_row
    return inverse * (scaled - lax.optimization_barrier(jnp.mean(scaled, axis=-1, keepdims=True)) - unit_rows * lax.optimization_barrier(jnp.mean(scaled * unit_rows, axis=-1, keepdims=True)))

def group_product(left, right):
    groups = N_DP * N_TENSOR
    row_count = left.shape[0]
    width = right.shape[0] // groups
    left_split = into_lone_copy(left).reshape(row_count, groups, width)
    right_split = into_lone_copy(right).reshape(groups, width, right.shape[1])
    partials = jnp.einsum('rgw,gwd->grd', left_split, right_split)
    return lax.optimization_barrier(jnp.sum(into_lone_copy(as_half(partials)), axis=0))

def group_input_grad(projection_gradient, query_key_value_nearby):
    groups = N_DP * N_TENSOR
    row_count = projection_gradient.shape[1]
    width = query_key_value_nearby.shape[2] // groups
    grad_split = into_lone_copy(projection_gradient).reshape(3, row_count, groups, width)
    weight_split = into_lone_copy(query_key_value_nearby).reshape(3, query_key_value_nearby.shape[1], groups, width)
    partials = jnp.einsum('trgw,tdgw->grd', grad_split, weight_split)
    return lax.optimization_barrier(jnp.sum(into_lone_copy(as_half(partials)), axis=0))

def attend(normalized_halves, query_key_value_nearby, gain_pair):
    row_count = normalized_halves.shape[0]
    image_count = row_count // PATCHES
    head_count = query_key_value_nearby.shape[2] // HS
    split_shape = (image_count, PATCHES, head_count, HS)
    query_raw = jnp.dot(normalized_halves, query_key_value_nearby[0], preferred_element_type=jnp.float32).reshape(split_shape)
    keys_raw = jnp.dot(normalized_halves, query_key_value_nearby[1], preferred_element_type=jnp.float32).reshape(split_shape)
    values_raw = jnp.dot(normalized_halves, query_key_value_nearby[2], preferred_element_type=jnp.float32).reshape(split_shape)
    query_normed, query_unit, query_inverse = norm_last(query_raw, gain_pair[0])
    key_normed, key_unit, key_inverse = norm_last(keys_raw, gain_pair[1])
    query_half = as_half(query_normed)
    key_half = as_half(key_normed)
    value_half = as_half(values_raw)
    scores = jnp.einsum('iphe,iqhe->ihpq', into_lone_copy(query_half), into_lone_copy(key_half)) / math.sqrt(HS)
    exponent = jnp.exp(scores)
    softmax_probs = exponent / lax.optimization_barrier(jnp.sum(exponent, axis=-1, keepdims=True))
    probs_half = as_half(softmax_probs)
    mixed_values = jnp.einsum('ihpq,iqhe->iphe', into_lone_copy(probs_half), into_lone_copy(value_half))
    attention = mixed_values.astype(jnp.bfloat16).reshape(row_count, head_count * HS)
    saved_state = (query_unit, query_inverse, key_unit, key_inverse, query_half, key_half, value_half, softmax_probs, probs_half)
    return (attention, saved_state)

def attend_back(grad_attention, saved_state, gain_pair):
    query_unit, query_inverse, key_unit, key_inverse, query_half, key_half, value_half, softmax_probs, probs_half = saved_state
    image_count, patch_count, head_count, head_size = query_half.shape
    grad_mixed = into_lone_copy(as_half(grad_attention)).reshape(query_half.shape)
    grad_probs = jnp.einsum('iphe,iqhe->ihpq', grad_mixed, into_lone_copy(value_half))
    grad_value = jnp.einsum('ihpq,iphe->iqhe', into_lone_copy(probs_half), grad_mixed)
    grad_scores = softmax_probs * (grad_probs - lax.optimization_barrier(jnp.sum(softmax_probs * grad_probs, axis=-1, keepdims=True)))
    score_half = into_lone_copy(as_half(grad_scores / math.sqrt(HS)))
    grad_query = jnp.einsum('ihpq,iqhe->iphe', score_half, into_lone_copy(key_half))
    grad_key = jnp.einsum('ihpq,iphe->iqhe', score_half, into_lone_copy(query_half))
    grad_query = norm_back(grad_query, query_unit, query_inverse, gain_pair[0])
    grad_key = norm_back(grad_key, key_unit, key_inverse, gain_pair[1])
    joined = jnp.stack([grad_query, grad_key, grad_value]).reshape(3, image_count * patch_count, head_count * head_size)
    return as_half(joined)

def layer_forward(rows_in, query_key_value_nearby, out_local, gain_row, gain_pair, grouped):
    normed, unit_rows, inverse = norm_last(into_lone_copy(rows_in), gain_row)
    normalized_halves = as_half(normed)
    attention, saved_state = attend(normalized_halves, query_key_value_nearby, gain_pair)
    if grouped:
        branch = group_product(attention, out_local)
    else:
        branch = jnp.dot(attention, out_local, preferred_element_type=jnp.float32)
    return (into_lone_copy(rows_in) + branch, (normalized_halves, unit_rows, inverse, attention, saved_state))

def section_forward(operands):
    rows_in, query_key_value_nearby, out_local, gain_row, gain_pair = operands
    return layer_forward(rows_in, query_key_value_nearby, out_local, gain_row, gain_pair, True)[0].astype(jnp.bfloat16)

def section_margin(operands):
    rows_in, query_key_value_nearby, out_local, gain_row, gain_pair, pool_row, head_local, label_row = operands
    summed, stash = layer_forward(rows_in, query_key_value_nearby, out_local, gain_row, gain_pair, False)
    normalized_halves, unit_rows, inverse, attention, saved_state = stash
    image_count = label_row.shape[0]
    model_width = summed.shape[1]
    pooled = lax.optimization_barrier(jnp.mean(summed.reshape(image_count, PATCHES, model_width), axis=1))
    pooled_normed, pooled_unit, pooled_inverse = norm_last(pooled, pool_row)
    pooled_half = as_half(pooled_normed)
    logits = jnp.dot(pooled_half, head_local, preferred_element_type=jnp.float32)
    targets = (label_row[:, None] == jnp.arange(CLASSES, dtype=jnp.int32)[None, :]).astype(jnp.float32)
    losses = lax.optimization_barrier(jnp.mean(jax.nn.softplus(logits) - targets * logits, axis=-1))
    grad_logits = as_half((jax.nn.sigmoid(logits) - targets) / image_count)
    grad_head = jnp.dot(pooled_half.T, grad_logits, preferred_element_type=jnp.float32)
    grad_pooled = norm_back(jnp.dot(grad_logits, head_local.T, preferred_element_type=jnp.float32), pooled_unit, pooled_inverse, pool_row)
    grad_image = grad_pooled / PATCHES
    grad_rows = jnp.broadcast_to(grad_image[:, None, :], (image_count, PATCHES, model_width)).reshape(summed.shape)
    grad_rows_half = as_half(grad_rows)
    grad_out = jnp.dot(attention.T, grad_rows_half, preferred_element_type=jnp.float32)
    grad_attention = jnp.dot(grad_rows_half, out_local.T, preferred_element_type=jnp.float32)
    projection_gradient = attend_back(grad_attention, saved_state, gain_pair)
    query_key_value_gradient = jnp.einsum('bp,sbn->spn', into_lone_copy(normalized_halves), into_lone_copy(projection_gradient))
    grad_normed = group_input_grad(projection_gradient, query_key_value_nearby)
    grad_inputs = as_half(grad_rows + norm_back(grad_normed, unit_rows, inverse, gain_row))
    return (grad_inputs, query_key_value_gradient, grad_out, grad_head, losses)

def section_own(operands):
    rows_in, query_key_value_nearby, out_local, gain_row, gain_pair, returned = operands
    stash = layer_forward(rows_in, query_key_value_nearby, out_local, gain_row, gain_pair, False)[1]
    normalized_halves, unit_rows, inverse, attention, saved_state = stash
    grad_out = jnp.dot(attention.T, returned, preferred_element_type=jnp.float32)
    grad_attention = jnp.dot(returned, out_local.T, preferred_element_type=jnp.float32)
    projection_gradient = attend_back(grad_attention, saved_state, gain_pair)
    query_key_value_gradient = jnp.einsum('bp,sbn->spn', into_lone_copy(normalized_halves), into_lone_copy(projection_gradient))
    return (query_key_value_gradient, grad_out)

def reference(block_inputs, qkv_weights, out_weights, norm_gain, query_key_gain, pool_gain, class_head, labels):
    out_rows = lax.map(section_forward, (block_inputs, qkv_weights, out_weights, norm_gain, query_key_gain))
    margin_in = jnp.concatenate([block_inputs[:1], out_rows[:-1]], axis=0)
    grad_inputs, qkv_first, out_first, grad_head, losses = lax.map(section_margin, (margin_in, qkv_weights, out_weights, norm_gain, query_key_gain, pool_gain, class_head, labels))
    returned = jnp.concatenate([grad_inputs[1:], jnp.zeros_like(grad_inputs[:1])], axis=0)
    qkv_second, out_second = lax.map(section_own, (block_inputs, qkv_weights, out_weights, norm_gain, query_key_gain, returned))
    query_key_value_gradient = (qkv_first + qkv_second).astype(jnp.bfloat16)
    grad_out = (out_first + out_second).astype(jnp.bfloat16)
    return (out_rows, query_key_value_gradient, grad_out, grad_head.astype(jnp.bfloat16), losses)
```

```python
import functools
import math

import jax
import jax.numpy as jnp
from jax import lax
from jax.experimental import pallas as pl
from jax.experimental.pallas import tpu as pltpu
from jax.sharding import PartitionSpec as P

HS = 128
PATCHES = 256
EPS = 1e-06
N_DP = 4
N_T = 2
ROWS = 64
TOTAL = 512
D = 3072
F = 384
CLASSES = 512
W = 512
CHUNKS = D // W
KINDS = ("A", "B", "A", "A", "B", "A")
MESH = pl.DeviceIdType.MESH
f32 = jnp.float32
bf16 = jnp.bfloat16
VM = pl.BlockSpec(memory_space=pltpu.VMEM)
ANY = pl.BlockSpec(memory_space=pl.ANY)


def dot_nn(a, b):
    return lax.dot_general(a, b, (((1,), (0,)), ((), ())), preferred_element_type=f32)


def dot_nt(a, b):
    return lax.dot_general(a, b, (((1,), (1,)), ((), ())), preferred_element_type=f32)


def norm_last(values, gain_row):
    centered = values - jnp.mean(values, axis=-1, keepdims=True)
    inverse = lax.rsqrt(jnp.mean(centered * centered, axis=-1, keepdims=True) + EPS)
    unit_rows = centered * inverse
    return unit_rows * gain_row, unit_rows, inverse


def norm_back(grad, unit_rows, inverse, gain_row):
    scaled = grad * gain_row
    return inverse * (
        scaled
        - jnp.mean(scaled, axis=-1, keepdims=True)
        - unit_rows * jnp.mean(scaled * unit_rows, axis=-1, keepdims=True)
    )


def place():
    return lax.axis_index("dp"), lax.axis_index("tensor")


def neighbour(dz, dt):
    z, t = place()
    target = {}
    if dz:
        target["dp"] = lax.rem(z + dz + N_DP, N_DP)
    if dt:
        target["tensor"] = 1 - t
    return target


def section_at(step):
    s, n = lax.axis_index("section"), lax.axis_size("section")
    return {"section": lax.rem(s + step + n, n)}


def enter(devices):
    barrier = pltpu.get_barrier_semaphore()
    for device in devices:
        pl.semaphore_signal(barrier, inc=1, device_id=device, device_id_type=MESH)
    pl.semaphore_wait(barrier, len(devices))


def rows_of(dz, dt):
    z, t = place()
    owner = lax.rem(z + dz + N_DP, N_DP) * N_T + ((1 - t) if dt else t)
    return pl.ds(pl.multiple_of(owner * ROWS, ROWS), ROWS)


def columns(c):
    return pl.ds(c * W, W)


class Gather:
    def __init__(self, buf, send_sem, recv_sem):
        self.buf, self.send_sem, self.recv_sem = buf, send_sem, recv_sem
        self.sent = []

    def view(self, dz, dt, c):
        return self.buf.at[rows_of(dz, dt), columns(c)]

    def send(self, c, dz, dt, to_z, to_t):
        k = sum(1 for (cc, _) in self.sent if cc == c)
        slot = ((dz - to_z) % N_DP) * 2 + (dt ^ to_t)
        part = self.view(dz, dt, c)
        copy = pltpu.make_async_remote_copy(
            src_ref=part,
            dst_ref=part,
            send_sem=self.send_sem.at[c, k],
            recv_sem=self.recv_sem.at[c, slot],
            device_id=neighbour(to_z, to_t),
            device_id_type=MESH,
        )
        copy.start()
        self.sent.append((c, copy))

    def recv(self, c, dz, dt):
        part = self.view(dz, dt, c)
        pltpu.make_async_remote_copy(
            src_ref=part,
            dst_ref=part,
            send_sem=self.send_sem.at[c, 0],
            recv_sem=self.recv_sem.at[c, (dz % N_DP) * 2 + dt],
            device_id=neighbour(1, 0),
            device_id_type=MESH,
        ).wait_recv()

    def begin(self, c):
        if KINDS[c] == "A":
            self.send(c, 0, 0, 0, 1)
            self.send(c, 0, 0, 1, 0)
            self.send(c, 0, 0, -1, 0)
        else:
            self.send(c, 0, 0, 1, 0)
            self.send(c, 0, 0, -1, 0)
            self.send(c, 0, 0, 0, 1)

    def first(self, c):
        if KINDS[c] == "A":
            self.recv(c, 0, 1)
            self.send(c, 0, 1, 1, 0)
            self.send(c, 0, 1, -1, 0)
            self.recv(c, -1, 0)
            self.send(c, -1, 0, 1, 0)
        else:
            way = 1 if c % 2 else -1
            self.recv(c, -way, 0)
            self.send(c, -way, 0, way, 0)
            self.send(c, -way, 0, 0, 1)
            self.recv(c, way, 0)
            self.send(c, way, 0, 0, 1)

    def second(self, c):
        if KINDS[c] == "A":
            self.recv(c, 1, 1)
            self.send(c, 1, 1, -1, 0)
        else:
            self.recv(c, 2, 0)
            self.send(c, 2, 0, 0, 1)

    def third(self, c):
        if KINDS[c] == "A":
            rest = ((1, 0), (-1, 1), (2, 0), (2, 1))
        else:
            rest = ((0, 1), (-1, 1), (1, 1), (2, 1))
        for dz, dt in rest:
            self.recv(c, dz, dt)

    def run(self, compute):
        for c in range(CHUNKS):
            self.begin(c)
        for i in range(CHUNKS + 2):
            if i < CHUNKS:
                self.first(i)
            if 0 <= i - 1 < CHUNKS:
                self.second(i - 1)
            if i >= 2:
                self.third(i - 2)
                compute(i - 2)

    def finish(self):
        for _, copy in self.sent:
            copy.wait_send()


RING = ((1, 0), (-1, 0), (0, 1))


class Scatter:
    def __init__(self, part, land, send_sem, recv_sem):
        self.part, self.land = part, land
        self.send_sem, self.recv_sem = send_sem, recv_sem
        self.sent = []

    def view(self, dz, dt, c):
        return self.part.at[rows_of(dz, dt), columns(c)]

    def send(self, c, dz, dt, to_z, to_t, slot):
        copy = pltpu.make_async_remote_copy(
            src_ref=self.view(dz, dt, c),
            dst_ref=self.land.at[c, slot],
            send_sem=self.send_sem.at[c, slot],
            recv_sem=self.recv_sem.at[c, slot],
            device_id=neighbour(to_z, to_t),
            device_id_type=MESH,
        )
        copy.start()
        self.sent.append(copy)

    def recv(self, c, slot):
        pltpu.make_async_remote_copy(
            src_ref=self.view(0, 0, c),
            dst_ref=self.land.at[c, slot],
            send_sem=self.send_sem.at[c, slot],
            recv_sem=self.recv_sem.at[c, slot],
            device_id=neighbour(1, 0),
            device_id_type=MESH,
        ).wait_recv()
        return self.land[c, slot].astype(f32)

    def value(self, dz, dt, c):
        return self.part[rows_of(dz, dt), columns(c)].astype(f32)

    def put(self, dz, dt, c, value):
        self.part[rows_of(dz, dt), columns(c)] = value.astype(bf16)

    def begin(self, c):
        if KINDS[c] == "A":
            self.send(c, 2, 0, 1, 0, 0)
            self.send(c, 2, 1, -1, 0, 1)
            self.send(c, -1, 0, -1, 0, 2)
            self.send(c, 1, 1, 1, 0, 3)
        else:
            self.send(c, 2, 1, 0, 1, 0)
            self.send(c, 1, 1, 0, 1, 1)
            self.send(c, -1, 1, 0, 1, 2)
            self.send(c, 0, 1, 0, 1, 3)

    def first(self, c):
        if KINDS[c] == "A":
            self.put(1, 0, c, self.value(1, 0, c) + self.recv(c, 0))
            self.send(c, 1, 0, 1, 0, 4)
            self.put(-1, 1, c, self.value(-1, 1, c) + self.recv(c, 1))
            self.send(c, -1, 1, -1, 0, 5)
        else:
            way = 1 if c % 2 else -1
            self.put(2, 0, c, self.value(2, 0, c) + self.recv(c, 0))
            self.send(c, 2, 0, way, 0, 4)
            other = 2 if way == 1 else 1
            self.put(-way, 0, c, self.value(-way, 0, c) + self.recv(c, other))
            self.send(c, -way, 0, -way, 0, 5)

    def second(self, c):
        if KINDS[c] == "A":
            total = self.value(0, 1, c) + self.recv(c, 3) + self.recv(c, 5)
            self.put(0, 1, c, total)
            self.send(c, 0, 1, 0, 1, 6)
        else:
            way = 1 if c % 2 else -1
            other = 1 if way == 1 else 2
            total = self.value(way, 0, c) + self.recv(c, other) + self.recv(c, 4)
            self.put(way, 0, c, total)
            self.send(c, way, 0, way, 0, 6)

    def third(self, c):
        rest = (2, 4, 6) if KINDS[c] == "A" else (3, 5, 6)
        total = self.value(0, 0, c)
        for slot in rest:
            total = total + self.recv(c, slot)
        return total

    def run(self, compute, done):
        for i in range(CHUNKS + 3):
            if i < CHUNKS:
                compute(i)
                self.begin(i)
            if 0 <= i - 1 < CHUNKS:
                self.first(i - 1)
            if 0 <= i - 2 < CHUNKS:
                self.second(i - 2)
            if 0 <= i - 3:
                done(i - 3, self.third(i - 3))

    def finish(self):
        for copy in self.sent:
            copy.wait_send()


def project_kernel(
    rows_ref, gain_ref, w_hbm, proj_ref, turned_ref, buf, wbuf, wsem, send_sem, recv_sem
):
    load = pltpu.make_async_copy(w_hbm, wbuf, wsem)
    load.start()
    normed, _, _ = norm_last(rows_ref[...].astype(f32), gain_ref[...])
    buf[rows_of(0, 0), :] = normed.astype(bf16)
    enter([neighbour(*way) for way in RING])
    gather = Gather(buf, send_sem, recv_sem)

    def compute(c):
        if c == 0:
            load.wait()

        def tile(r, carry):
            rows = pl.ds(pl.multiple_of(r * 256, 256), 256)
            block = buf[rows, columns(c)]
            for t in range(3):
                value = dot_nn(block, wbuf[t, columns(c), :])
                cols = pl.ds(t * F, F)
                if c == 0:
                    proj_ref[rows, cols] = value
                else:
                    proj_ref[rows, cols] += value
            turned_ref[columns(c), rows] = block.T
            return carry

        lax.fori_loop(0, TOTAL // 256, tile, 0)

    gather.run(compute)
    gather.finish()


def params(collective_id=None, limit=60 * 1024 * 1024):
    if collective_id is None:
        return pltpu.CompilerParams(vmem_limit_bytes=limit)
    return pltpu.CompilerParams(
        collective_id=collective_id, has_side_effects=True, vmem_limit_bytes=limit
    )


def ring_sems():
    return [pltpu.SemaphoreType.DMA((CHUNKS, 8)), pltpu.SemaphoreType.DMA((CHUNKS, 8))]


def project(rows, gain_row, qkv_local, collective_id):
    return pl.pallas_call(
        project_kernel,
        out_shape=(
            jax.ShapeDtypeStruct((TOTAL, 3 * F), f32),
            jax.ShapeDtypeStruct((D, TOTAL), bf16),
        ),
        in_specs=[VM, VM, ANY],
        out_specs=(VM, VM),
        scratch_shapes=[
            pltpu.VMEM((TOTAL, D), bf16),
            pltpu.VMEM((3, D, F), bf16),
            pltpu.SemaphoreType.DMA,
        ]
        + ring_sems(),
        compiler_params=params(collective_id),
        name=f"project_{collective_id}",
    )(rows, gain_row, qkv_local)


def head_state(q_ref, k_ref, v_ref, pair_ref):
    q_normed, q_unit, q_inv = norm_last(q_ref[...], pair_ref[0:1, :])
    k_normed, k_unit, k_inv = norm_last(k_ref[...], pair_ref[1:2, :])
    q_half, k_half = q_normed.astype(bf16), k_normed.astype(bf16)
    v_half = v_ref[...].astype(bf16)
    exponent = jnp.exp(dot_nt(q_half, k_half) * (1.0 / math.sqrt(HS)))
    probs = exponent * (1.0 / jnp.sum(exponent, axis=-1, keepdims=True))
    return q_unit, q_inv, k_unit, k_inv, q_half, k_half, v_half, probs


def attend_kernel(q_ref, k_ref, v_ref, pair_ref, att_ref, turned_ref):
    v_half, probs = head_state(q_ref, k_ref, v_ref, pair_ref)[-2:]
    mixed = dot_nn(probs.astype(bf16), v_half)
    att_ref[...] = mixed.astype(bf16)
    turned_ref[...] = mixed.T.astype(bf16)


def qkv_specs():
    return [
        pl.BlockSpec((PATCHES, HS), lambda i, h, t=t: (i, 3 * t + h)) for t in range(3)
    ] + [pl.BlockSpec((2, HS), lambda i, h: (0, 0))]


def attend(projected, gain_pair):
    return pl.pallas_call(
        attend_kernel,
        grid=(2, 3),
        out_shape=(
            jax.ShapeDtypeStruct((TOTAL, F), bf16),
            jax.ShapeDtypeStruct((F, TOTAL), bf16),
        ),
        in_specs=qkv_specs(),
        out_specs=(
            pl.BlockSpec((PATCHES, HS), lambda i, h: (i, h)),
            pl.BlockSpec((HS, PATCHES), lambda i, h: (h, i)),
        ),
        compiler_params=params(),
        name="attend",
    )(projected, projected, projected, gain_pair)


def attend_back_kernel(shared, q_ref, k_ref, v_ref, pair_ref, grad_ref, out_ref):
    q_unit, q_inv, k_unit, k_inv, q_half, k_half, v_half, probs = head_state(
        q_ref, k_ref, v_ref, pair_ref
    )
    if shared:
        row = grad_ref[pl.ds(pl.program_id(0), 1), :]
        mixed = jnp.broadcast_to(row, (PATCHES, HS)).astype(bf16)
    else:
        mixed = grad_ref[...].astype(bf16)
    grad_probs = dot_nt(mixed, v_half)
    probs_t = probs.T.astype(bf16)
    grad_value = dot_nn(probs_t, mixed)
    grad_scores = probs * (grad_probs - jnp.sum(probs * grad_probs, axis=-1, keepdims=True))
    scaled = grad_scores * (1.0 / math.sqrt(HS))
    score_half = scaled.astype(bf16)
    grad_query = dot_nn(score_half, k_half)
    grad_key = dot_nn(scaled.T.astype(bf16), q_half)
    out_ref[0] = norm_back(grad_query, q_unit, q_inv, pair_ref[0:1, :]).astype(bf16)
    out_ref[1] = norm_back(grad_key, k_unit, k_inv, pair_ref[1:2, :]).astype(bf16)
    out_ref[2] = grad_value.astype(bf16)


def attend_back(projected, gain_pair, grad, shared):
    if shared:
        grad_spec = pl.BlockSpec((8, HS), lambda i, h: (0, h))
    else:
        grad_spec = pl.BlockSpec((PATCHES, HS), lambda i, h: (i, h))
    return pl.pallas_call(
        functools.partial(attend_back_kernel, shared),
        grid=(2, 3),
        out_shape=jax.ShapeDtypeStruct((3, TOTAL, F), bf16),
        in_specs=qkv_specs() + [grad_spec],
        out_specs=pl.BlockSpec((3, PATCHES, HS), lambda i, h: (0, i, h)),
        compiler_params=params(),
        name="attend_back",
    )(projected, projected, projected, gain_pair, grad)


def out_kernel(
    att_ref,
    w_ref,
    rows_ref,
    out_ref,
    margin_ref,
    part,
    land,
    next_rows,
    send_sem,
    recv_sem,
    step_send,
    step_recv,
):
    enter(
        [neighbour(*way) for way in RING] + [section_at(1), section_at(-1)]
    )
    scatter = Scatter(part, land, send_sem, recv_sem)
    hops = []

    def compute(c):
        def tile(r, carry):
            rows = pl.ds(pl.multiple_of(r * 256, 256), 256)
            part[rows, columns(c)] = dot_nn(att_ref[rows, :], w_ref[:, columns(c)]).astype(bf16)
            return carry

        lax.fori_loop(0, TOTAL // 256, tile, 0)

    def done(c, total):
        out_ref[:, columns(c)] = (rows_ref[:, columns(c)].astype(f32) + total).astype(bf16)
        copy = pltpu.make_async_remote_copy(
            src_ref=out_ref.at[:, columns(c)],
            dst_ref=next_rows.at[:, columns(c)],
            send_sem=step_send.at[c],
            recv_sem=step_recv.at[c],
            device_id=section_at(1),
            device_id_type=MESH,
        )
        copy.start()
        hops.append(copy)

    scatter.run(compute, done)
    for copy in hops:
        copy.wait_recv()
    first = lax.axis_index("section") == 0
    margin_ref[...] = jnp.where(first, rows_ref[...], next_rows[...])
    scatter.finish()
    for copy in hops:
        copy.wait_send()


def land_scratch():
    return [pltpu.VMEM((TOTAL, D), bf16), pltpu.VMEM((CHUNKS, 7, ROWS, W), bf16)]


def out_rows(attention, out_local, rows, collective_id):
    return pl.pallas_call(
        out_kernel,
        out_shape=(jax.ShapeDtypeStruct((ROWS, D), bf16), jax.ShapeDtypeStruct((ROWS, D), bf16)),
        in_specs=[VM, VM, VM],
        out_specs=(VM, VM),
        scratch_shapes=land_scratch()
        + [pltpu.VMEM((ROWS, D), bf16)]
        + ring_sems()
        + [pltpu.SemaphoreType.DMA((CHUNKS,)), pltpu.SemaphoreType.DMA((CHUNKS,))],
        compiler_params=params(collective_id),
        name="out_rows",
    )(attention, out_local, rows)


PEERS = tuple((dz, dt) for dz in range(N_DP) for dt in range(N_T) if dz or dt)
PACK = D // 4


def pack_rows(ref, value):
    for i in range(2):
        for q in range(4):
            ref[i * 4 + q : i * 4 + q + 1, :] = value[i : i + 1, q * PACK : (q + 1) * PACK]


def head_kernel(
    att_ref,
    w_ref,
    rows_ref,
    label_ref,
    pool_ref,
    head_hbm,
    loss_ref,
    head_grad_ref,
    image_ref,
    per_image_ref,
    sums_ref,
    head,
    stage,
    land,
    pooled_ref,
    half_ref,
    head_sem,
    send_sem,
    recv_sem,
):
    load = pltpu.make_async_copy(head_hbm, head, head_sem)
    load.start()
    row_id = lax.broadcasted_iota(jnp.int32, (8, 1), 0)
    sums_ref[...] = jnp.zeros_like(sums_ref)
    for i in range(2):
        block = att_ref[i * PATCHES : (i + 1) * PATCHES, :].astype(f32)
        sums_ref[i : i + 1, :] = jnp.sum(block, axis=0, keepdims=True)
    sums = sums_ref[...]
    hi = sums.astype(bf16)
    rest = sums - hi.astype(f32)
    mid = rest.astype(bf16)
    low = (rest - mid.astype(f32)).astype(bf16)
    w_out = w_ref[...]
    partial_rows = dot_nn(hi, w_out) + dot_nn(mid, w_out) + dot_nn(low, w_out)
    own = jnp.sum(rows_ref[...].astype(f32), axis=0, keepdims=True)
    image = lax.axis_index("dp") // (N_DP // 2)
    partial_rows = partial_rows + jnp.where(row_id == image, own, 0.0)
    pack_rows(stage, partial_rows)
    enter([neighbour(*way) for way in PEERS])
    copies = []
    for k, way in enumerate(PEERS):
        copy = pltpu.make_async_remote_copy(
            src_ref=stage,
            dst_ref=land.at[k],
            send_sem=send_sem.at[k],
            recv_sem=recv_sem.at[k],
            device_id=neighbour(*way),
            device_id_type=MESH,
        )
        copy.start()
        copies.append(copy)
    load.wait()
    total = stage[...]
    for k, copy in enumerate(copies):
        copy.wait_recv()
        total = total + land[k]
    pooled_ref[...] = jnp.zeros_like(pooled_ref)
    for i in range(2):
        for q in range(4):
            pooled_ref[i : i + 1, q * PACK : (q + 1) * PACK] = total[i * 4 + q : i * 4 + q + 1, :]
    pooled = pooled_ref[...] / PATCHES
    gain = pool_ref[...]
    normed, unit_rows, inverse = norm_last(pooled, gain)
    half = normed.astype(bf16)
    half_ref[...] = half.astype(f32)
    logits = dot_nn(half, head[...])
    targets = (label_ref[...] == lax.broadcasted_iota(jnp.int32, (8, CLASSES), 1)).astype(f32)
    soft = jnp.maximum(logits, 0.0) + jnp.log1p(jnp.exp(-jnp.abs(logits)))
    loss = jnp.mean(soft - targets * logits, axis=-1, keepdims=True)
    loss_ref[...] = jnp.broadcast_to(loss, loss_ref.shape)
    grad_logits = (jax.nn.sigmoid(logits) - targets) / 2
    grad_logits = jnp.where(row_id < 2, grad_logits, 0.0).astype(bf16)
    z, t = place()
    width = D // (N_DP * N_T)
    start = pl.multiple_of((z * N_T + t) * width, width)
    mine = half_ref[:, pl.ds(start, width)]
    head_grad_ref[...] = dot_nn(mine.T.astype(bf16), grad_logits).astype(bf16)
    grad_pooled = norm_back(dot_nt(grad_logits, head[...]), unit_rows, inverse, gain)
    grad_image = grad_pooled / PATCHES
    image_ref[...] = jnp.where(row_id < 2, grad_image, 0.0)
    per_image_ref[...] = dot_nt(grad_image.astype(bf16), w_out)
    for copy in copies:
        copy.wait_send()


def classify(attention, out_local, margin_rows, labels8, pool_row, head_local, collective_id):
    return pl.pallas_call(
        head_kernel,
        out_shape=(
            jax.ShapeDtypeStruct((8, 128), f32),
            jax.ShapeDtypeStruct((F, CLASSES), bf16),
            jax.ShapeDtypeStruct((8, D), f32),
            jax.ShapeDtypeStruct((8, F), f32),
            jax.ShapeDtypeStruct((8, F), f32),
        ),
        in_specs=[VM, VM, VM, VM, VM, ANY],
        out_specs=(VM,) * 5,
        scratch_shapes=[
            pltpu.VMEM((D, CLASSES), bf16),
            pltpu.VMEM((8, PACK), f32),
            pltpu.VMEM((len(PEERS), 8, PACK), f32),
            pltpu.VMEM((8, D), f32),
            pltpu.VMEM((8, D), f32),
            pltpu.SemaphoreType.DMA,
            pltpu.SemaphoreType.DMA((len(PEERS),)),
            pltpu.SemaphoreType.DMA((len(PEERS),)),
        ],
        compiler_params=params(collective_id),
        name="classify",
    )(attention, out_local, margin_rows, labels8, pool_row, head_local)


def input_grad_kernel(
    grad_ref,
    w_hbm,
    rows_ref,
    gain_ref,
    image_ref,
    back_ref,
    part,
    land,
    wbuf,
    total_ref,
    mine,
    came,
    wsem,
    send_sem,
    recv_sem,
    step_send,
    step_recv,
):
    loads = []
    for c in range(CHUNKS):
        load = pltpu.make_async_copy(
            w_hbm.at[:, columns(c), :], wbuf.at[:, columns(c), :], wsem.at[c]
        )
        load.start()
        loads.append(load)
    enter([neighbour(*way) for way in RING] + [section_at(1), section_at(-1)])
    scatter = Scatter(part, land, send_sem, recv_sem)

    def compute(c):
        loads[c].wait()

        def tile(r, carry):
            rows = pl.ds(pl.multiple_of(r * 256, 256), 256)
            value = dot_nt(grad_ref[0, rows, :], wbuf[0, columns(c), :])
            value = value + dot_nt(grad_ref[1, rows, :], wbuf[1, columns(c), :])
            value = value + dot_nt(grad_ref[2, rows, :], wbuf[2, columns(c), :])
            part[rows, columns(c)] = value.astype(bf16)
            return carry

        lax.fori_loop(0, TOTAL // 256, tile, 0)

    def done(c, total):
        total_ref[:, columns(c)] = total

    scatter.run(compute, done)
    gain = gain_ref[...]
    _, unit_rows, inverse = norm_last(rows_ref[...].astype(f32), gain)
    image = lax.axis_index("dp") // (N_DP // 2)
    residual = jnp.where(image == 0, image_ref[0:1, :], image_ref[1:2, :])
    grad = residual + norm_back(total_ref[...], unit_rows, inverse, gain)
    mine[...] = grad.astype(bf16)
    copies = []
    for c in range(2):
        part_columns = pl.ds(c * (D // 2), D // 2)
        copy = pltpu.make_async_remote_copy(
            src_ref=mine.at[:, part_columns],
            dst_ref=came.at[:, part_columns],
            send_sem=step_send.at[c],
            recv_sem=step_recv.at[c],
            device_id=section_at(-1),
            device_id_type=MESH,
        )
        copy.start()
        copies.append(copy)
    scatter.finish()
    for copy in copies:
        copy.wait_recv()
    last = lax.axis_index("section") == lax.axis_size("section") - 1
    back_ref[...] = jnp.where(last, jnp.zeros_like(came), came[...])
    for copy in copies:
        copy.wait_send()


def input_grads(projection_gradient, qkv_local, margin_rows, gain_row, grad_image, collective_id):
    return pl.pallas_call(
        input_grad_kernel,
        out_shape=jax.ShapeDtypeStruct((ROWS, D), bf16),
        in_specs=[VM, ANY, VM, VM, VM],
        out_specs=VM,
        scratch_shapes=land_scratch()
        + [
            pltpu.VMEM((3, D, F), bf16),
            pltpu.VMEM((ROWS, D), f32),
            pltpu.VMEM((ROWS, D), bf16),
            pltpu.VMEM((ROWS, D), bf16),
            pltpu.SemaphoreType.DMA((CHUNKS,)),
        ]
        + ring_sems()
        + [pltpu.SemaphoreType.DMA((2,)), pltpu.SemaphoreType.DMA((2,))],
        compiler_params=params(collective_id),
        name="input_grads",
    )(projection_gradient, qkv_local, margin_rows, gain_row, grad_image)


def cotangent_kernel(
    rows_ref,
    w_ref,
    turned_ref,
    sums_ref,
    image_ref,
    margin_turned_ref,
    margin_grad_ref,
    grad_att_ref,
    grad_out_ref,
    margin_part_ref,
    buf,
    send_sem,
    recv_sem,
):
    buf[rows_of(0, 0), :] = rows_ref[...]
    enter([neighbour(*way) for way in RING])
    gather = Gather(buf, send_sem, recv_sem)
    sums = sums_ref[...]
    hi = sums.T.astype(bf16)
    low = (sums.T - hi.astype(f32)).astype(bf16)

    def compute(c):
        def tile(r, carry):
            rows = pl.ds(pl.multiple_of(r * 256, 256), 256)
            value = dot_nt(buf[rows, columns(c)], w_ref[:, columns(c)])
            if c == 0:
                grad_att_ref[rows, :] = value
            else:
                grad_att_ref[rows, :] += value
            return carry

        lax.fori_loop(0, TOTAL // 256, tile, 0)
        shared = image_ref[:, columns(c)].astype(bf16)
        value = dot_nn(turned_ref[...], buf[:, columns(c)])
        value = value + dot_nn(hi, shared) + dot_nn(low, shared)
        grad_out_ref[:, columns(c)] = value.astype(bf16)

        def margin_tile(r, carry):
            rows = pl.ds(pl.multiple_of(c * W + r * 256, 256), 256)
            for t in range(3):
                margin_part_ref[t, rows, :] = dot_nn(
                    margin_turned_ref[rows, :], margin_grad_ref[t]
                ).astype(bf16)
            return carry

        lax.fori_loop(0, W // 256, margin_tile, 0)

    gather.run(compute)
    gather.finish()


def cotangents(returned, out_local, turned, sums, grad_image, margin_turned, margin_grad, collective_id):
    return pl.pallas_call(
        cotangent_kernel,
        out_shape=(
            jax.ShapeDtypeStruct((TOTAL, F), f32),
            jax.ShapeDtypeStruct((F, D), bf16),
            jax.ShapeDtypeStruct((3, D, F), bf16),
        ),
        in_specs=[VM] * 7,
        out_specs=(VM,) * 3,
        scratch_shapes=[pltpu.VMEM((TOTAL, D), bf16)] + ring_sems(),
        compiler_params=params(collective_id),
        name="cotangents",
    )(returned, out_local, turned, sums, grad_image, margin_turned, margin_grad)


def weight_kernel(turned_ref, grad_ref, part_ref, out_ref):
    value = dot_nn(turned_ref[...], grad_ref[0]) + part_ref[0].astype(f32)
    out_ref[0] = value.astype(bf16)


def weight_grads(turned, projection_gradient, margin_part):
    tall = 768
    return pl.pallas_call(
        weight_kernel,
        grid=(D // tall, 3),
        out_shape=jax.ShapeDtypeStruct((3, D, F), bf16),
        in_specs=[
            pl.BlockSpec((tall, TOTAL), lambda r, t: (r, 0)),
            pl.BlockSpec((1, TOTAL, F), lambda r, t: (t, 0, 0)),
            pl.BlockSpec((1, tall, F), lambda r, t: (t, r, 0)),
        ],
        out_specs=pl.BlockSpec((1, tall, F), lambda r, t: (t, r, 0)),
        compiler_params=params(),
        name="weight_grads",
    )(turned, projection_gradient, margin_part)


def on_device(
    block_inputs, qkv_weights, out_weights, norm_gain, query_key_gain, pool_gain, class_head, labels
):
    rows_in, qkv_local, out_local = block_inputs[0], qkv_weights[0], out_weights[0]
    gain_pair = query_key_gain[0]
    labels8 = jnp.broadcast_to(jnp.pad(labels[0], (0, 6))[:, None], (8, CLASSES))

    projected_own, turned_own = project(rows_in, norm_gain, qkv_local, 0)
    attention_own, attention_turned = attend(projected_own, gain_pair)
    out_own, margin_rows = out_rows(attention_own, out_local, rows_in, 1)

    projected, turned = project(margin_rows, norm_gain, qkv_local, 2)
    attention, _ = attend(projected, gain_pair)
    losses, grad_head, grad_image, per_image, sums = classify(
        attention, out_local, margin_rows, labels8, pool_gain, class_head[0], 3
    )
    margin_grad = attend_back(projected, gain_pair, per_image, True)
    returned = input_grads(margin_grad, qkv_local, margin_rows, norm_gain, grad_image, 4)

    grad_attention, grad_out, margin_part = cotangents(
        returned, out_local, attention_turned, sums, grad_image, turned, margin_grad, 5
    )
    own_grad = attend_back(projected_own, gain_pair, grad_attention, False)
    qkv_grad = weight_grads(turned_own, own_grad, margin_part)
    return (
        out_own[None],
        qkv_grad[None],
        grad_out[None],
        grad_head[None],
        losses[:2, 0][None],
    )


def solution(mesh):
    in_specs = (
        P("section", ("dp", "tensor"), None),
        P("section", None, None, ("dp", "tensor")),
        P("section", ("dp", "tensor"), None),
        P("section", None),
        P("section", None, None),
        P("section", None),
        P("section", None, None),
        P("section", None),
    )
    out_specs = (
        P("section", ("dp", "tensor"), None),
        P("section", None, None, ("dp", "tensor")),
        P("section", ("dp", "tensor"), None),
        P("section", ("dp", "tensor"), None),
        P("section", None),
    )
    return jax.shard_map(
        on_device, mesh=mesh, in_specs=in_specs, out_specs=out_specs, check_vma=False
    )
```

```python
import functools
import math

import jax
import jax.numpy as jnp
from jax import lax
from jax.experimental import pallas as pl
from jax.experimental.pallas import tpu as pltpu
from jax.sharding import PartitionSpec as P

HS = 128
PATCHES = 256
EPS = 1e-06
N_DP = 4
N_T = 2
ROWS = 64
TOTAL = 512
D = 3072
F = 384
CLASSES = 512
W = 512
CHUNKS = D // W
AHEAD = 2
KINDS = ("A", "B", "A", "A", "B", "A")
MESH = pl.DeviceIdType.MESH
f32 = jnp.float32
bf16 = jnp.bfloat16
VM = pl.BlockSpec(memory_space=pltpu.VMEM)
ANY = pl.BlockSpec(memory_space=pl.ANY)


def dot_nn(a, b):
    return lax.dot_general(a, b, (((1,), (0,)), ((), ())), preferred_element_type=f32)


def dot_nt(a, b):
    return lax.dot_general(a, b, (((1,), (1,)), ((), ())), preferred_element_type=f32)


def norm_last(values, gain_row):
    centered = values - jnp.mean(values, axis=-1, keepdims=True)
    inverse = lax.rsqrt(jnp.mean(centered * centered, axis=-1, keepdims=True) + EPS)
    unit_rows = centered * inverse
    return unit_rows * gain_row, unit_rows, inverse


def norm_back(grad, unit_rows, inverse, gain_row):
    scaled = grad * gain_row
    return inverse * (
        scaled
        - jnp.mean(scaled, axis=-1, keepdims=True)
        - unit_rows * jnp.mean(scaled * unit_rows, axis=-1, keepdims=True)
    )


def place():
    return lax.axis_index("dp"), lax.axis_index("tensor")


def neighbour(dz, dt):
    z, t = place()
    target = {}
    if dz:
        target["dp"] = lax.rem(z + dz + N_DP, N_DP)
    if dt:
        target["tensor"] = 1 - t
    return target


def section_at(step):
    s, n = lax.axis_index("section"), lax.axis_size("section")
    return {"section": lax.rem(s + step + n, n)}


def enter(devices):
    barrier = pltpu.get_barrier_semaphore()
    for device in devices:
        pl.semaphore_signal(barrier, inc=1, device_id=device, device_id_type=MESH)
    pl.semaphore_wait(barrier, len(devices))


def rows_of(dz, dt):
    z, t = place()
    owner = lax.rem(z + dz + N_DP, N_DP) * N_T + ((1 - t) if dt else t)
    return pl.ds(pl.multiple_of(owner * ROWS, ROWS), ROWS)


def columns(c):
    return pl.ds(c * W, W)


class Gather:
    def __init__(self, buf, send_sem, recv_sem):
        self.buf, self.send_sem, self.recv_sem = buf, send_sem, recv_sem
        self.sent = []

    def view(self, dz, dt, c):
        return self.buf.at[rows_of(dz, dt), columns(c)]

    def send(self, c, dz, dt, to_z, to_t):
        k = sum(1 for (cc, _) in self.sent if cc == c)
        slot = ((dz - to_z) % N_DP) * 2 + (dt ^ to_t)
        part = self.view(dz, dt, c)
        copy = pltpu.make_async_remote_copy(
            src_ref=part,
            dst_ref=part,
            send_sem=self.send_sem.at[c, k],
            recv_sem=self.recv_sem.at[c, slot],
            device_id=neighbour(to_z, to_t),
            device_id_type=MESH,
        )
        copy.start()
        self.sent.append((c, copy))

    def recv(self, c, dz, dt):
        part = self.view(dz, dt, c)
        pltpu.make_async_remote_copy(
            src_ref=part,
            dst_ref=part,
            send_sem=self.send_sem.at[c, 0],
            recv_sem=self.recv_sem.at[c, (dz % N_DP) * 2 + dt],
            device_id=neighbour(1, 0),
            device_id_type=MESH,
        ).wait_recv()

    def begin(self, c):
        if KINDS[c] == "A":
            self.send(c, 0, 0, 0, 1)
            self.send(c, 0, 0, 1, 0)
            self.send(c, 0, 0, -1, 0)
        else:
            self.send(c, 0, 0, 1, 0)
            self.send(c, 0, 0, -1, 0)
            self.send(c, 0, 0, 0, 1)

    def first(self, c):
        if KINDS[c] == "A":
            self.recv(c, 0, 1)
            self.send(c, 0, 1, 1, 0)
            self.send(c, 0, 1, -1, 0)
            self.recv(c, -1, 0)
            self.send(c, -1, 0, 1, 0)
        else:
            way = 1 if c % 2 else -1
            self.recv(c, -way, 0)
            self.send(c, -way, 0, way, 0)
            self.send(c, -way, 0, 0, 1)
            self.recv(c, way, 0)
            self.send(c, way, 0, 0, 1)

    def second(self, c):
        if KINDS[c] == "A":
            self.recv(c, 1, 1)
            self.send(c, 1, 1, -1, 0)
        else:
            self.recv(c, 2, 0)
            self.send(c, 2, 0, 0, 1)

    def third(self, c):
        if KINDS[c] == "A":
            rest = ((1, 0), (-1, 1), (2, 0), (2, 1))
        else:
            rest = ((0, 1), (-1, 1), (1, 1), (2, 1))
        for dz, dt in rest:
            self.recv(c, dz, dt)

    def run(self, compute, side=None):
        for c in range(AHEAD):
            self.begin(c)
        for i in range(CHUNKS + 2):
            if i < CHUNKS:
                self.first(i)
            if i + AHEAD < CHUNKS:
                self.begin(i + AHEAD)
            if side is not None:
                side(i)
            if 0 <= i - 1 < CHUNKS:
                self.second(i - 1)
            if i >= 2:
                self.third(i - 2)
                compute(i - 2)

    def finish(self):
        for _, copy in self.sent:
            copy.wait_send()


RING = ((1, 0), (-1, 0), (0, 1))


class Scatter:
    def __init__(self, part, land, send_sem, recv_sem):
        self.part, self.land = part, land
        self.send_sem, self.recv_sem = send_sem, recv_sem
        self.sent = []

    def view(self, dz, dt, c):
        return self.part.at[rows_of(dz, dt), columns(c)]

    def send(self, c, dz, dt, to_z, to_t, slot):
        copy = pltpu.make_async_remote_copy(
            src_ref=self.view(dz, dt, c),
            dst_ref=self.land.at[c, slot],
            send_sem=self.send_sem.at[c, slot],
            recv_sem=self.recv_sem.at[c, slot],
            device_id=neighbour(to_z, to_t),
            device_id_type=MESH,
        )
        copy.start()
        self.sent.append(copy)

    def recv(self, c, slot):
        pltpu.make_async_remote_copy(
            src_ref=self.view(0, 0, c),
            dst_ref=self.land.at[c, slot],
            send_sem=self.send_sem.at[c, slot],
            recv_sem=self.recv_sem.at[c, slot],
            device_id=neighbour(1, 0),
            device_id_type=MESH,
        ).wait_recv()
        return self.land[c, slot].astype(f32)

    def value(self, dz, dt, c):
        return self.part[rows_of(dz, dt), columns(c)].astype(f32)

    def put(self, dz, dt, c, value):
        self.part[rows_of(dz, dt), columns(c)] = value.astype(bf16)

    def begin(self, c):
        if KINDS[c] == "A":
            self.send(c, 2, 0, 1, 0, 0)
            self.send(c, 2, 1, -1, 0, 1)
            self.send(c, -1, 0, -1, 0, 2)
            self.send(c, 1, 1, 1, 0, 3)
        else:
            self.send(c, 2, 1, 0, 1, 0)
            self.send(c, 1, 1, 0, 1, 1)
            self.send(c, -1, 1, 0, 1, 2)
            self.send(c, 0, 1, 0, 1, 3)

    def first(self, c):
        if KINDS[c] == "A":
            self.put(1, 0, c, self.value(1, 0, c) + self.recv(c, 0))
            self.send(c, 1, 0, 1, 0, 4)
            self.put(-1, 1, c, self.value(-1, 1, c) + self.recv(c, 1))
            self.send(c, -1, 1, -1, 0, 5)
        else:
            way = 1 if c % 2 else -1
            self.put(2, 0, c, self.value(2, 0, c) + self.recv(c, 0))
            self.send(c, 2, 0, way, 0, 4)
            other = 2 if way == 1 else 1
            self.put(-way, 0, c, self.value(-way, 0, c) + self.recv(c, other))
            self.send(c, -way, 0, -way, 0, 5)

    def second(self, c):
        if KINDS[c] == "A":
            total = self.value(0, 1, c) + self.recv(c, 3) + self.recv(c, 5)
            self.put(0, 1, c, total)
            self.send(c, 0, 1, 0, 1, 6)
        else:
            way = 1 if c % 2 else -1
            other = 1 if way == 1 else 2
            total = self.value(way, 0, c) + self.recv(c, other) + self.recv(c, 4)
            self.put(way, 0, c, total)
            self.send(c, way, 0, way, 0, 6)

    def third(self, c):
        rest = (2, 4, 6) if KINDS[c] == "A" else (3, 5, 6)
        total = self.value(0, 0, c)
        for slot in rest:
            total = total + self.recv(c, slot)
        return total

    def run(self, compute, done):
        for i in range(CHUNKS + 3):
            if i < CHUNKS:
                compute(i)
                self.begin(i)
            if 0 <= i - 1 < CHUNKS:
                self.first(i - 1)
            if 0 <= i - 2 < CHUNKS:
                self.second(i - 2)
            if 0 <= i - 3:
                done(i - 3, self.third(i - 3))

    def finish(self):
        for copy in self.sent:
            copy.wait_send()


def params(collective_id=None, limit=62 * 1024 * 1024):
    if collective_id is None:
        return pltpu.CompilerParams(vmem_limit_bytes=limit)
    return pltpu.CompilerParams(
        collective_id=collective_id, has_side_effects=True, vmem_limit_bytes=limit
    )


def ring_sems():
    return [pltpu.SemaphoreType.DMA((CHUNKS, 8)), pltpu.SemaphoreType.DMA((CHUNKS, 8))]


def land_scratch():
    return [pltpu.VMEM((TOTAL, D), bf16), pltpu.VMEM((CHUNKS, 7, ROWS, W), bf16)]


def image_rows(i):
    return pl.ds(pl.multiple_of(i * PATCHES, PATCHES), PATCHES)


def project_chunk(buf, wbuf, proj, turned, c):
    def tile(r, carry):
        rows = image_rows(r)
        block = buf[rows, columns(c)]
        for t in range(3):
            value = dot_nn(block, wbuf[t, columns(c), :])
            cols = pl.ds(t * F, F)
            if c == 0:
                proj[rows, cols] = value
            else:
                proj[rows, cols] += value
        turned[columns(c), rows] = block.T
        return carry

    lax.fori_loop(0, TOTAL // PATCHES, tile, 0)


def head_cols(t, h):
    return pl.ds(t * F + h * HS, HS)


def head_state(q, k, v, pair):
    q_normed, q_unit, q_inv = norm_last(q, pair[0:1, :])
    k_normed, k_unit, k_inv = norm_last(k, pair[1:2, :])
    q_half, k_half = q_normed.astype(bf16), k_normed.astype(bf16)
    v_half = v.astype(bf16)
    exponent = jnp.exp(dot_nt(q_half, k_half) * (1.0 / math.sqrt(HS)))
    probs = exponent * (1.0 / jnp.sum(exponent, axis=-1, keepdims=True))
    return q_unit, q_inv, k_unit, k_inv, q_half, k_half, v_half, probs


def state_of(proj, pair, rows, h):
    return head_state(*[proj[rows, head_cols(t, h)] for t in range(3)], pair)


def attend(proj, pair_ref, att, turned):
    def image(i, carry):
        rows = image_rows(i)
        for h in range(3):
            v_half, probs = state_of(proj, pair_ref[...], rows, h)[-2:]
            mixed = dot_nn(probs.astype(bf16), v_half)
            att[rows, pl.ds(h * HS, HS)] = mixed.astype(bf16)
            if turned is not None:
                turned[pl.ds(h * HS, HS), rows] = mixed.T.astype(bf16)
        return carry

    lax.fori_loop(0, 2, image, 0)


def back_of_head(state, pair, mixed):
    q_unit, q_inv, k_unit, k_inv, q_half, k_half, v_half, probs = state
    grad_probs = dot_nt(mixed, v_half)
    grad_value = dot_nn(probs.T.astype(bf16), mixed)
    grad_scores = probs * (grad_probs - jnp.sum(probs * grad_probs, axis=-1, keepdims=True))
    scaled = grad_scores * (1.0 / math.sqrt(HS))
    grad_query = dot_nn(scaled.astype(bf16), k_half)
    grad_key = dot_nn(scaled.T.astype(bf16), q_half)
    return (
        norm_back(grad_query, q_unit, q_inv, pair[0:1, :]).astype(bf16),
        norm_back(grad_key, k_unit, k_inv, pair[1:2, :]).astype(bf16),
        grad_value.astype(bf16),
    )


PEERS = tuple((dz, dt) for dz in range(N_DP) for dt in range(N_T) if dz or dt)
PACK = D // 4


def front_kernel(
    rows_ref,
    gain_ref,
    pair_ref,
    pool_ref,
    label_ref,
    w_hbm,
    wout_hbm,
    head_hbm,
    out_ref,
    margin_ref,
    proj_hbm,
    turned_hbm,
    att_turned_ref,
    margin_turned_hbm,
    margin_grad_ref,
    head_grad_ref,
    image_ref,
    sums_ref,
    loss_ref,
    wbuf,
    wout,
    head,
    buf_own,
    buf_margin,
    proj_own,
    proj_margin,
    turned_own,
    turned_margin,
    att,
    part,
    land,
    next_rows,
    stage,
    pool_land,
    pooled_ref,
    half_ref,
    per_image,
    load_sem,
    store_sem,
    own_send,
    own_recv,
    sum_send,
    sum_recv,
    step_send,
    step_recv,
    margin_send,
    margin_recv,
    pool_send,
    pool_recv,
):
    load_w = pltpu.make_async_copy(w_hbm, wbuf, load_sem.at[0])
    load_out = pltpu.make_async_copy(wout_hbm, wout, load_sem.at[1])
    load_head = pltpu.make_async_copy(head_hbm, head, load_sem.at[2])
    load_w.start()
    load_out.start()
    load_head.start()
    normed, _, _ = norm_last(rows_ref[...].astype(f32), gain_ref[...])
    buf_own[rows_of(0, 0), :] = normed.astype(bf16)
    enter([neighbour(*way) for way in PEERS] + [section_at(1), section_at(-1)])

    gather = Gather(buf_own, own_send, own_recv)

    def compute_own(c):
        if c == 0:
            load_w.wait()
        project_chunk(buf_own, wbuf, proj_own, turned_own, c)

    gather.run(compute_own)
    stores = [
        pltpu.make_async_copy(proj_own, proj_hbm, store_sem.at[0]),
        pltpu.make_async_copy(turned_own, turned_hbm, store_sem.at[1]),
    ]
    for store in stores:
        store.start()
    attend(proj_own, pair_ref, att, att_turned_ref)

    load_out.wait()
    scatter = Scatter(part, land, sum_send, sum_recv)
    hops = []

    def out_chunk(c):
        def tile(r, carry):
            rows = image_rows(r)
            part[rows, columns(c)] = dot_nn(att[rows, :], wout[:, columns(c)]).astype(bf16)
            return carry

        lax.fori_loop(0, TOTAL // PATCHES, tile, 0)

    def out_done(c, total):
        out_ref[:, columns(c)] = (rows_ref[:, columns(c)].astype(f32) + total).astype(bf16)
        copy = pltpu.make_async_remote_copy(
            src_ref=out_ref.at[:, columns(c)],
            dst_ref=next_rows.at[:, columns(c)],
            send_sem=step_send.at[c],
            recv_sem=step_recv.at[c],
            device_id=section_at(1),
            device_id_type=MESH,
        )
        copy.start()
        hops.append(copy)

    scatter.run(out_chunk, out_done)
    for copy in hops:
        copy.wait_recv()
    first = lax.axis_index("section") == 0
    margin = jnp.where(first, rows_ref[...], next_rows[...])
    margin_ref[...] = margin
    normed, _, _ = norm_last(margin.astype(f32), gain_ref[...])
    buf_margin[rows_of(0, 0), :] = normed.astype(bf16)
    second = Gather(buf_margin, margin_send, margin_recv)
    second.run(lambda c: project_chunk(buf_margin, wbuf, proj_margin, turned_margin, c))
    store = pltpu.make_async_copy(turned_margin, margin_turned_hbm, store_sem.at[2])
    store.start()
    stores.append(store)
    attend(proj_margin, pair_ref, att, None)

    row_id = lax.broadcasted_iota(jnp.int32, (8, 1), 0)
    sums_ref[...] = jnp.zeros_like(sums_ref)
    for i in range(2):
        block = att[i * PATCHES : (i + 1) * PATCHES, :].astype(f32)
        sums_ref[i : i + 1, :] = jnp.sum(block, axis=0, keepdims=True)
    sums = sums_ref[...]
    hi = sums.astype(bf16).astype(f32)
    mid = (sums - hi).astype(bf16).astype(f32)
    low = sums - hi - mid
    tall = jnp.concatenate([hi, mid, low], axis=0).astype(bf16)
    terms = dot_nn(tall, wout[...])
    partial_rows = terms[0:8] + terms[8:16] + terms[16:24]
    own = jnp.sum(margin_ref[...].astype(f32), axis=0, keepdims=True)
    image = lax.axis_index("dp") // (N_DP // 2)
    partial_rows = partial_rows + jnp.where(row_id == image, own, 0.0)
    for i in range(2):
        for q in range(4):
            stage[i * 4 + q : i * 4 + q + 1, :] = partial_rows[i : i + 1, q * PACK : (q + 1) * PACK]
    copies = []
    for k, way in enumerate(PEERS):
        copy = pltpu.make_async_remote_copy(
            src_ref=stage,
            dst_ref=pool_land.at[k],
            send_sem=pool_send.at[k],
            recv_sem=pool_recv.at[k],
            device_id=neighbour(*way),
            device_id_type=MESH,
        )
        copy.start()
        copies.append(copy)
    load_head.wait()
    total = stage[...]
    for k, copy in enumerate(copies):
        copy.wait_recv()
        total = total + pool_land[k]
    pooled_ref[...] = jnp.zeros_like(pooled_ref)
    for i in range(2):
        for q in range(4):
            pooled_ref[i : i + 1, q * PACK : (q + 1) * PACK] = total[i * 4 + q : i * 4 + q + 1, :]
    gain = pool_ref[...]
    normed, unit_rows, inverse = norm_last(pooled_ref[...] / PATCHES, gain)
    half = normed.astype(bf16)
    half_ref[...] = half.astype(f32)
    logits = dot_nn(half, head[...])
    label = jnp.where(row_id == 0, label_ref[0:1, 0:1], label_ref[0:1, 1:2])
    targets = (label == lax.broadcasted_iota(jnp.int32, (8, CLASSES), 1)).astype(f32)
    soft = jnp.maximum(logits, 0.0) + jnp.log1p(jnp.exp(-jnp.abs(logits)))
    loss = jnp.mean(soft - targets * logits, axis=-1, keepdims=True)
    lane = lax.broadcasted_iota(jnp.int32, (8, 128), 1)
    loss_ref[...] = jnp.sum(jnp.where(row_id == lane, loss, 0.0), axis=0, keepdims=True)[:, 0:2]
    grad_logits = (jax.nn.sigmoid(logits) - targets) / 2
    grad_logits = jnp.where(row_id < 2, grad_logits, 0.0).astype(bf16)
    grad_pooled = norm_back(dot_nt(grad_logits, head[...]), unit_rows, inverse, gain)
    grad_image = grad_pooled / PATCHES
    image_ref[...] = jnp.where(row_id < 2, grad_image, 0.0)
    per_image[...] = dot_nt(grad_image.astype(bf16), wout[...])
    z, t = place()
    width = D // (N_DP * N_T)
    start = pl.multiple_of((z * N_T + t) * width, width)
    mine = half_ref[:, pl.ds(start, width)]
    head_grad_ref[...] = dot_nn(mine.T.astype(bf16), grad_logits).astype(bf16)

    def back_image(i, carry):
        rows = image_rows(i)
        for h in range(3):
            state = state_of(proj_margin, pair_ref[...], rows, h)
            row = jnp.where(i == 0, per_image[0:1, pl.ds(h * HS, HS)], per_image[1:2, pl.ds(h * HS, HS)])
            mixed = jnp.broadcast_to(row, (PATCHES, HS)).astype(bf16)
            for t, value in enumerate(back_of_head(state, pair_ref[...], mixed)):
                margin_grad_ref[t, rows, pl.ds(h * HS, HS)] = value
        return carry

    lax.fori_loop(0, 2, back_image, 0)
    gather.finish()
    scatter.finish()
    second.finish()
    for copy in hops + copies:
        copy.wait_send()
    for store in stores:
        store.wait()


def front(rows, gain_row, gain_pair, pool_row, labels, qkv_local, out_local, head_local, collective_id):
    return pl.pallas_call(
        front_kernel,
        out_shape=(
            jax.ShapeDtypeStruct((ROWS, D), bf16),
            jax.ShapeDtypeStruct((ROWS, D), bf16),
            jax.ShapeDtypeStruct((TOTAL, 3 * F), f32),
            jax.ShapeDtypeStruct((D, TOTAL), bf16),
            jax.ShapeDtypeStruct((F, TOTAL), bf16),
            jax.ShapeDtypeStruct((D, TOTAL), bf16),
            jax.ShapeDtypeStruct((3, TOTAL, F), bf16),
            jax.ShapeDtypeStruct((F, CLASSES), bf16),
            jax.ShapeDtypeStruct((8, D), f32),
            jax.ShapeDtypeStruct((8, F), f32),
            jax.ShapeDtypeStruct((1, 2), f32),
        ),
        in_specs=[VM, VM, VM, VM, VM, ANY, ANY, ANY],
        out_specs=(VM, VM, ANY, ANY, VM, ANY, VM, VM, VM, VM, VM),
        scratch_shapes=[
            pltpu.VMEM((3, D, F), bf16),
            pltpu.VMEM((F, D), bf16),
            pltpu.VMEM((D, CLASSES), bf16),
            pltpu.VMEM((TOTAL, D), bf16),
            pltpu.VMEM((TOTAL, D), bf16),
            pltpu.VMEM((TOTAL, 3 * F), f32),
            pltpu.VMEM((TOTAL, 3 * F), f32),
            pltpu.VMEM((D, TOTAL), bf16),
            pltpu.VMEM((D, TOTAL), bf16),
            pltpu.VMEM((TOTAL, F), bf16),
        ]
        + land_scratch()
        + [
            pltpu.VMEM((ROWS, D), bf16),
            pltpu.VMEM((8, PACK), f32),
            pltpu.VMEM((len(PEERS), 8, PACK), f32),
            pltpu.VMEM((8, D), f32),
            pltpu.VMEM((8, D), f32),
            pltpu.VMEM((8, F), f32),
            pltpu.SemaphoreType.DMA((3,)),
            pltpu.SemaphoreType.DMA((3,)),
        ]
        + ring_sems()
        + ring_sems()
        + [pltpu.SemaphoreType.DMA((CHUNKS,)), pltpu.SemaphoreType.DMA((CHUNKS,))]
        + ring_sems()
        + [pltpu.SemaphoreType.DMA((len(PEERS),)), pltpu.SemaphoreType.DMA((len(PEERS),))],
        compiler_params=params(collective_id),
        name="front",
    )(rows, gain_row, gain_pair, pool_row, labels, qkv_local, out_local, head_local)


def back_kernel(
    grad_ref,
    rows_ref,
    gain_ref,
    image_ref,
    sums_ref,
    w_hbm,
    wout_hbm,
    turned_hbm,
    margin_turned_hbm,
    grad_att_ref,
    grad_out_hbm,
    margin_part_hbm,
    part,
    land,
    wbuf,
    wout,
    turned,
    margin_turned,
    total_ref,
    mine,
    came,
    buf,
    grad_out,
    margin_part,
    wsem,
    load_sem,
    out_sem,
    part_sem,
    sum_send,
    sum_recv,
    step_send,
    step_recv,
    own_send,
    own_recv,
):
    loads = []
    for c in range(CHUNKS):
        load = pltpu.make_async_copy(
            w_hbm.at[:, columns(c), :], wbuf.at[:, columns(c), :], wsem.at[c]
        )
        load.start()
        loads.append(load)
    later = [
        pltpu.make_async_copy(margin_turned_hbm, margin_turned, load_sem.at[0]),
        pltpu.make_async_copy(wout_hbm, wout, load_sem.at[1]),
        pltpu.make_async_copy(turned_hbm, turned, load_sem.at[2]),
    ]
    for load in later:
        load.start()
    enter([neighbour(*way) for way in RING] + [section_at(1), section_at(-1)])
    scatter = Scatter(part, land, sum_send, sum_recv)

    def compute(c):
        loads[c].wait()

        def tile(r, carry):
            rows = image_rows(r)
            value = dot_nt(grad_ref[0, rows, :], wbuf[0, columns(c), :])
            value = value + dot_nt(grad_ref[1, rows, :], wbuf[1, columns(c), :])
            value = value + dot_nt(grad_ref[2, rows, :], wbuf[2, columns(c), :])
            part[rows, columns(c)] = value.astype(bf16)
            return carry

        lax.fori_loop(0, TOTAL // PATCHES, tile, 0)

    def done(c, total):
        total_ref[:, columns(c)] = total

    scatter.run(compute, done)
    gain = gain_ref[...]
    _, unit_rows, inverse = norm_last(rows_ref[...].astype(f32), gain)
    image = lax.axis_index("dp") // (N_DP // 2)
    residual = jnp.where(image == 0, image_ref[0:1, :], image_ref[1:2, :])
    grad = residual + norm_back(total_ref[...], unit_rows, inverse, gain)
    mine[...] = grad.astype(bf16)
    copies = []
    for c in range(CHUNKS):
        copy = pltpu.make_async_remote_copy(
            src_ref=mine.at[:, columns(c)],
            dst_ref=came.at[:, columns(c)],
            send_sem=step_send.at[c],
            recv_sem=step_recv.at[c],
            device_id=section_at(-1),
            device_id_type=MESH,
        )
        copy.start()
        copies.append(copy)
    for load in later:
        load.wait()
    last = lax.axis_index("section") == lax.axis_size("section") - 1

    gather = Gather(buf, own_send, own_recv)
    begin = gather.begin

    def begin_after_hop(c):
        copies[c].wait_recv()
        block = came[:, columns(c)]
        buf[rows_of(0, 0), columns(c)] = jnp.where(last, jnp.zeros_like(block), block)
        begin(c)

    gather.begin = begin_after_hop
    sums_t = sums_ref[...].T
    hi = sums_t.astype(bf16)
    low = (sums_t - hi.astype(f32)).astype(bf16)
    stores = []

    def margin_piece(c):
        if c >= CHUNKS:
            return

        def margin_tile(r, carry):
            rows = pl.ds(pl.multiple_of(c * W + r * 256, 256), 256)
            for t in range(3):
                margin_part[t, rows, :] = dot_nn(margin_turned[rows, :], grad_ref[t]).astype(bf16)
            return carry

        lax.fori_loop(0, W // 256, margin_tile, 0)
        store = pltpu.make_async_copy(
            margin_part.at[:, columns(c), :], margin_part_hbm.at[:, columns(c), :], part_sem.at[c]
        )
        store.start()
        stores.append(store)

    def chunk(c):
        def tile(r, carry):
            rows = image_rows(r)
            value = dot_nt(buf[rows, columns(c)], wout[:, columns(c)])
            if c == 0:
                grad_att_ref[rows, :] = value
            else:
                grad_att_ref[rows, :] += value
            return carry

        lax.fori_loop(0, TOTAL // PATCHES, tile, 0)
        shared = image_ref[:, columns(c)].astype(bf16)
        value = dot_nn(turned[...], buf[:, columns(c)])
        value = value + dot_nn(hi, shared) + dot_nn(low, shared)
        grad_out[:, columns(c)] = value.astype(bf16)
        store = pltpu.make_async_copy(
            grad_out.at[:, columns(c)], grad_out_hbm.at[:, columns(c)], out_sem.at[c]
        )
        store.start()
        stores.append(store)

    gather.run(chunk, margin_piece)
    scatter.finish()
    gather.finish()
    for copy in copies:
        copy.wait_send()
    for store in stores:
        store.wait()


def back(grad, rows, gain_row, grad_image, sums, qkv_local, out_local, turned, margin_turned, collective_id):
    return pl.pallas_call(
        back_kernel,
        out_shape=(
            jax.ShapeDtypeStruct((TOTAL, F), f32),
            jax.ShapeDtypeStruct((F, D), bf16),
            jax.ShapeDtypeStruct((3, D, F), bf16),
        ),
        in_specs=[VM] * 5 + [ANY] * 4,
        out_specs=(VM, ANY, ANY),
        scratch_shapes=land_scratch()
        + [
            pltpu.VMEM((3, D, F), bf16),
            pltpu.VMEM((F, D), bf16),
            pltpu.VMEM((F, TOTAL), bf16),
            pltpu.VMEM((D, TOTAL), bf16),
            pltpu.VMEM((ROWS, D), f32),
            pltpu.VMEM((ROWS, D), bf16),
            pltpu.VMEM((ROWS, D), bf16),
            pltpu.VMEM((TOTAL, D), bf16),
            pltpu.VMEM((F, D), bf16),
            pltpu.VMEM((3, D, F), bf16),
            pltpu.SemaphoreType.DMA((CHUNKS,)),
            pltpu.SemaphoreType.DMA((3,)),
            pltpu.SemaphoreType.DMA((CHUNKS,)),
            pltpu.SemaphoreType.DMA((CHUNKS,)),
        ]
        + ring_sems()
        + [pltpu.SemaphoreType.DMA((CHUNKS,)), pltpu.SemaphoreType.DMA((CHUNKS,))]
        + ring_sems(),
        compiler_params=params(collective_id),
        name="back",
    )(grad, rows, gain_row, grad_image, sums, qkv_local, out_local, turned, margin_turned)


def own_back_kernel(proj_ref, pair_ref, grad_ref, out_ref):
    rows = pl.ds(0, PATCHES)
    for h in range(3):
        cols = pl.ds(h * HS, HS)
        state = state_of(proj_ref, pair_ref[...], rows, h)
        mixed = grad_ref[:, cols].astype(bf16)
        for t, value in enumerate(back_of_head(state, pair_ref[...], mixed)):
            out_ref[t, :, cols] = value


def own_back(projected, gain_pair, grad):
    return pl.pallas_call(
        own_back_kernel,
        grid=(2,),
        out_shape=jax.ShapeDtypeStruct((3, TOTAL, F), bf16),
        in_specs=[
            pl.BlockSpec((PATCHES, 3 * F), lambda i: (i, 0)),
            pl.BlockSpec((2, HS), lambda i: (0, 0)),
            pl.BlockSpec((PATCHES, F), lambda i: (i, 0)),
        ],
        out_specs=pl.BlockSpec((3, PATCHES, F), lambda i: (0, i, 0)),
        compiler_params=params(),
        name="own_back",
    )(projected, gain_pair, grad)


def weight_kernel(turned_ref, grad_ref, part_ref, *refs):
    count = len(refs) // 2
    passed, out_ref = refs[:count], refs[count]
    for t in range(3):
        value = dot_nn(turned_ref[...], grad_ref[t]) + part_ref[t].astype(f32)
        out_ref[t] = value.astype(bf16)
    for source, target in zip(passed, refs[count + 1 :]):
        target[...] = source[...]


def weight_grads(turned, projection_gradient, margin_part, passed):
    steps = 12
    tall = D // steps
    specs = [
        pl.BlockSpec((ROWS, D // steps), lambda r: (0, r)),
        pl.BlockSpec((F, D // steps), lambda r: (0, r)),
        pl.BlockSpec((F // steps, CLASSES), lambda r: (r, 0)),
    ]
    return pl.pallas_call(
        weight_kernel,
        grid=(steps,),
        out_shape=[jax.ShapeDtypeStruct((3, D, F), bf16)]
        + [jax.ShapeDtypeStruct(x.shape, x.dtype) for x in passed],
        in_specs=[
            pl.BlockSpec((tall, TOTAL), lambda r: (r, 0)),
            pl.BlockSpec((3, TOTAL, F), lambda r: (0, 0, 0)),
            pl.BlockSpec((3, tall, F), lambda r: (0, r, 0)),
        ]
        + specs,
        out_specs=[pl.BlockSpec((3, tall, F), lambda r: (0, r, 0))] + specs,
        compiler_params=params(),
        name="weight_grads",
    )(turned, projection_gradient, margin_part, *passed)


def on_device(
    block_inputs, qkv_weights, out_weights, norm_gain, query_key_gain, pool_gain, class_head, labels
):
    rows_in, qkv_local, out_local = block_inputs[0], qkv_weights[0], out_weights[0]
    gain_pair = query_key_gain[0]
    (
        out_own,
        margin_rows,
        projected,
        turned,
        attention_turned,
        margin_turned,
        margin_grad,
        grad_head,
        grad_image,
        sums,
        losses,
    ) = front(
        rows_in, norm_gain, gain_pair, pool_gain, labels, qkv_local, out_local, class_head[0], 0
    )
    grad_attention, grad_out, margin_part = back(
        margin_grad,
        margin_rows,
        norm_gain,
        grad_image,
        sums,
        qkv_local,
        out_local,
        attention_turned,
        margin_turned,
        1,
    )
    own_grad = own_back(projected, gain_pair, grad_attention)
    qkv_grad, out_own, grad_out, grad_head = weight_grads(
        turned, own_grad, margin_part, (out_own, grad_out, grad_head)
    )
    return (out_own[None], qkv_grad[None], grad_out[None], grad_head[None], losses)


def solution(mesh):
    in_specs = (
        P("section", ("dp", "tensor"), None),
        P("section", None, None, ("dp", "tensor")),
        P("section", ("dp", "tensor"), None),
        P("section", None),
        P("section", None, None),
        P("section", None),
        P("section", None, None),
        P("section", None),
    )
    out_specs = (
        P("section", ("dp", "tensor"), None),
        P("section", None, None, ("dp", "tensor")),
        P("section", ("dp", "tensor"), None),
        P("section", ("dp", "tensor"), None),
        P("section", None),
    )
    return jax.shard_map(
        on_device, mesh=mesh, in_specs=in_specs, out_specs=out_specs, check_vma=False
    )
```

```python
import functools
import math

import jax
import jax.numpy as jnp
from jax import lax
from jax.experimental import pallas as pl
from jax.experimental.pallas import tpu as pltpu
from jax.sharding import PartitionSpec as P

HS = 128
PATCHES = 256
EPS = 1e-06
N_DP = 4
N_T = 2
ROWS = 64
TOTAL = 512
D = 3072
F = 384
TALL = 512
STEPS = D // TALL
CLASSES = 512
PROJECT_PLAN = (('A', 768, (1, 1)), ('B', 1024, (-1,)), ('A', 256, (1, -1)), ('B', 256, (-1,)), ('B', 256, (1,)), ('A', 512, (-1, -1)))
PROJECT_STEPS = (
    (1, 0, 0, 0, 1), (1, 1, 0, 3, 0), (1, -1, 0, 1, 0), (1, 0, 1, 0, 1), (1, 1, 1, 3, 0), (1, -1, 1, 1, 0),
    (0, 0, 3, 0), (1, 1, 0, 2, 0), (0, 0, 1, 0), (1, 0, 2, 0, 1), (1, -1, 2, 1, 0), (0, 0, 0, 1),
    (1, 1, 0, 3, 1), (1, -1, 0, 1, 1), (1, 0, 3, 0, 1), (1, 0, 4, 0, 1), (1, 0, 5, 0, 1), (0, 1, 3, 0),
    (1, 0, 1, 3, 1), (0, 1, 1, 0), (1, -1, 1, 2, 0), (1, 0, 1, 1, 1), (0, 2, 1, 0), (0, 1, 0, 1),
    (0, 2, 0, 1), (1, 1, 2, 3, 1), (1, -1, 2, 1, 1), (0, 0, 2, 0), (0, 3, 0, 1), (1, 1, 2, 3, 0),
    (0, 0, 1, 1), (0, 4, 0, 1), (1, 1, 3, 3, 0), (1, 1, 4, 3, 0), (1, -1, 3, 1, 0), (0, 0, 3, 1),
    (1, 1, 0, 2, 1), (0, 5, 0, 1), (1, 1, 5, 3, 1), (1, -1, 5, 1, 1), (0, 2, 3, 1), (0, 2, 3, 0),
    (1, 1, 2, 2, 0), (0, 1, 2, 0), (1, 0, 1, 2, 1), (1, -1, 4, 1, 0), (0, 3, 3, 0), (1, 0, 3, 3, 1),
    (0, 2, 1, 1), (1, -1, 2, 2, 1), (0, 4, 3, 0), (1, 1, 4, 2, 0), (1, 0, 4, 3, 1), (0, 3, 1, 0),
    (1, -1, 3, 2, 0), (1, 0, 3, 1, 1), (0, 1, 3, 1), (1, -1, 5, 1, 0), (0, 5, 1, 1), (1, -1, 5, 2, 1),
    (0, 0, 2, 1), (2, 0, 0), (0, 4, 1, 0), (1, 0, 4, 1, 1), (0, 2, 2, 1), (0, 1, 1, 1),
    (1, 1, 5, 3, 0), (2, 0, 1), (0, 5, 3, 1), (0, 3, 2, 0), (1, 0, 3, 2, 1), (0, 2, 2, 0),
    (2, 2, 0), (2, 2, 1), (0, 4, 2, 0), (1, 0, 4, 2, 1), (0, 5, 1, 0), (1, -1, 5, 2, 0),
    (0, 1, 2, 1), (2, 1, 0), (0, 5, 3, 0), (0, 5, 2, 1), (0, 3, 3, 1), (2, 1, 1),
    (0, 4, 3, 1), (0, 3, 1, 1), (0, 5, 2, 0), (2, 5, 0), (0, 4, 1, 1), (2, 5, 1),
    (0, 3, 2, 1), (2, 3, 0), (2, 3, 1), (0, 4, 2, 1), (2, 4, 0), (2, 4, 1),
)
RETURN_PLAN = (('B', 256, (-1,)), ('B', 256, (1,)), ('A', 1024, (-1, 1)), ('B', 256, (-1,)), ('A', 768, (-1, 1)), ('B', 512, (1,)))
RETURN_STEPS = (
    (1, 1, 0, 3, 0), (1, -1, 0, 1, 0), (1, 0, 0, 0, 1), (1, 1, 1, 3, 0), (1, -1, 1, 1, 0), (1, 0, 1, 0, 1),
    (1, 0, 2, 0, 1), (1, 1, 2, 3, 0), (1, -1, 2, 1, 0), (1, 1, 3, 3, 0), (1, -1, 3, 1, 0), (1, 0, 3, 0, 1),
    (1, 0, 4, 0, 1), (1, 1, 4, 3, 0), (1, -1, 4, 1, 0), (3, 0), (3, 1), (0, 0, 3, 0),
    (1, 0, 0, 3, 1), (0, 0, 1, 0), (1, -1, 0, 2, 0), (1, 0, 0, 1, 1), (1, 1, 5, 3, 0), (1, -1, 5, 1, 0),
    (3, 2), (0, 1, 3, 0), (1, 1, 1, 2, 0), (1, 0, 1, 3, 1), (0, 1, 1, 0), (1, 0, 1, 1, 1),
    (0, 0, 0, 1), (3, 3), (0, 1, 0, 1), (3, 4), (1, 0, 5, 0, 1), (3, 5),
    (0, 2, 3, 0), (0, 2, 1, 0), (1, -1, 2, 2, 0), (3, 6), (0, 3, 3, 0), (1, 0, 3, 3, 1),
    (0, 3, 1, 0), (1, -1, 3, 2, 0), (1, 0, 3, 1, 1), (0, 2, 0, 1), (1, 1, 2, 3, 1), (1, -1, 2, 1, 1),
    (3, 7), (0, 3, 0, 1), (0, 4, 3, 0), (0, 4, 1, 0), (1, -1, 4, 2, 0), (0, 0, 2, 0),
    (1, 0, 0, 2, 1), (0, 4, 0, 1), (1, 1, 4, 3, 1), (1, -1, 4, 1, 1), (0, 5, 3, 0), (1, 1, 5, 2, 0),
    (1, 0, 5, 3, 1), (0, 0, 3, 1), (0, 1, 2, 0), (1, 0, 1, 2, 1), (0, 5, 1, 0), (1, 0, 5, 1, 1),
    (0, 0, 1, 1), (0, 1, 3, 1), (0, 1, 1, 1), (0, 2, 3, 1), (1, 1, 2, 2, 1), (0, 2, 2, 0),
    (0, 5, 0, 1), (0, 3, 2, 0), (1, 0, 3, 2, 1), (0, 3, 3, 1), (0, 3, 1, 1), (0, 4, 3, 1),
    (1, 1, 4, 2, 1), (0, 0, 2, 1), (2, 0, 0), (2, 0, 1), (0, 5, 2, 0), (1, 0, 5, 2, 1),
    (0, 2, 1, 1), (0, 5, 3, 1), (0, 1, 2, 1), (2, 1, 0), (2, 1, 1), (0, 4, 2, 0),
    (0, 5, 1, 1), (0, 2, 2, 1), (2, 2, 0), (0, 3, 2, 1), (2, 2, 1), (2, 3, 0),
    (0, 4, 1, 1), (2, 3, 1), (0, 5, 2, 1), (2, 5, 0), (2, 5, 1), (0, 4, 2, 1),
    (2, 4, 0), (2, 4, 1),
)
OUT_PLAN = (('A', 512, (1, 1)), ('A', 256, (1, 1)), ('B', 1280, (-1,)), ('A', 512, (-1, 1)), ('A', 512, (1, -1)))
OUT_STEPS = (
    (0, 0), (1, 0, 1, 0), (1, 0, 1, 1), (1, 0, -1, 2), (1, 0, -1, 3), (0, 1),
    (0, 2), (1, 2, 0, 0), (0, 3), (1, 1, 1, 0), (1, 1, -1, 2), (0, 4),
    (1, 1, 1, 1), (1, 1, -1, 3), (1, 3, 1, 1), (1, 2, 0, 1), (1, 3, -1, 0), (2, 0, (0,), 1, 4),
    (1, 3, -1, 3), (2, 0, (1,), 1, 5), (1, 4, -1, 1), (2, 1, (0,), 1, 4), (1, 2, 0, 2), (2, 1, (1,), 1, 5),
    (1, 4, -1, 2), (2, 2, (0,), -1, 4), (2, 3, (1,), 1, 5), (2, 3, (0,), -1, 4), (1, 3, 1, 2), (1, 2, 0, 3),
    (2, 0, (3, 5), 0, 6), (2, 4, (1,), -1, 5), (1, 4, 1, 0), (2, 1, (3, 5), 0, 6), (1, 4, 1, 3), (2, 3, (3, 5), 0, 6),
    (2, 2, (2,), 1, 5), (2, 2, (1, 4), -1, 6), (2, 4, (0,), 1, 4), (2, 4, (3, 5), 0, 6), (2, 0, (2, 4, 6), None, None), (2, 1, (2, 4, 6), None, None),
    (2, 3, (2, 4, 6), None, None), (2, 2, (3, 5, 6), None, None), (2, 4, (2, 4, 6), None, None),
)
INPUT_PLAN = (('B', 256, (-1,)), ('A', 768, (-1, 1)), ('B', 256, (1,)), ('B', 1024, (1,)), ('A', 512, (1, -1)), ('A', 256, (-1, -1)))
INPUT_STEPS = (
    (0, 0), (1, 0, 0, 0), (1, 0, 0, 1), (1, 0, 0, 2), (1, 0, 0, 3), (0, 1),
    (1, 1, -1, 0), (1, 1, 1, 1), (1, 1, 1, 2), (1, 1, -1, 3), (0, 2), (1, 2, 0, 0),
    (1, 2, 0, 1), (1, 2, 0, 2), (1, 2, 0, 3), (0, 3), (2, 0, (0,), -1, 4), (2, 0, (2,), 1, 5),
    (1, 3, 0, 0), (1, 3, 0, 1), (1, 3, 0, 2), (1, 3, 0, 3), (0, 4), (2, 1, (0,), -1, 4),
    (2, 1, (1,), 1, 5), (2, 2, (0,), 1, 4), (1, 4, 1, 0), (1, 4, -1, 1), (1, 4, -1, 2), (1, 4, 1, 3),
    (0, 5), (2, 2, (2,), -1, 5), (1, 5, -1, 0), (1, 5, -1, 1), (1, 5, 1, 2), (1, 5, 1, 3),
    (2, 0, (1, 4), -1, 6), (2, 3, (0,), 1, 4), (2, 1, (3, 5), 0, 6), (2, 2, (1, 4), 1, 6), (2, 4, (1,), -1, 5), (2, 4, (0,), 1, 4),
    (2, 5, (0,), -1, 4), (2, 5, (1,), -1, 5), (2, 0, (3, 5, 6), None, None), (2, 3, (2,), -1, 5), (2, 4, (3, 5), 0, 6), (2, 3, (1, 4), 1, 6),
    (2, 5, (3, 5), 0, 6), (2, 2, (3, 5, 6), None, None), (2, 1, (2, 4, 6), None, None), (2, 4, (2, 4, 6), None, None), (2, 5, (2, 4, 6), None, None), (2, 3, (3, 5, 6), None, None),
)
MESH = pl.DeviceIdType.MESH
f32 = jnp.float32
bf16 = jnp.bfloat16
VM = pl.BlockSpec(memory_space=pltpu.VMEM)
ANY = pl.BlockSpec(memory_space=pl.ANY)


def dot_nn(a, b):
    return lax.dot_general(a, b, (((1,), (0,)), ((), ())), preferred_element_type=f32)


def dot_nt(a, b):
    return lax.dot_general(a, b, (((1,), (1,)), ((), ())), preferred_element_type=f32)


def norm_last(values, gain_row):
    centered = values - jnp.mean(values, axis=-1, keepdims=True)
    inverse = lax.rsqrt(jnp.mean(centered * centered, axis=-1, keepdims=True) + EPS)
    unit_rows = centered * inverse
    return unit_rows * gain_row, unit_rows, inverse


def norm_back(grad, unit_rows, inverse, gain_row):
    scaled = grad * gain_row
    return inverse * (
        scaled
        - jnp.mean(scaled, axis=-1, keepdims=True)
        - unit_rows * jnp.mean(scaled * unit_rows, axis=-1, keepdims=True)
    )


def place():
    return lax.axis_index("dp"), lax.axis_index("tensor")


def neighbour(dz, dt):
    z, t = place()
    target = {}
    if dz:
        target["dp"] = lax.rem(z + dz + N_DP, N_DP)
    if dt:
        target["tensor"] = 1 - t
    return target


def section_at(step):
    s, n = lax.axis_index("section"), lax.axis_size("section")
    return {"section": lax.rem(s + step + n, n)}


def greet(devices):
    barrier = pltpu.get_barrier_semaphore()
    for device in devices:
        pl.semaphore_signal(barrier, inc=1, device_id=device, device_id_type=MESH)


def enter(devices):
    pl.semaphore_wait(pltpu.get_barrier_semaphore(), len(devices))


def rows_of(dz, dt):
    z, t = place()
    owner = lax.rem(z + dz + N_DP, N_DP) * N_T + ((1 - t) if dt else t)
    return pl.ds(pl.multiple_of(owner * ROWS, ROWS), ROWS)


class Plan:
    def __init__(self, plan):
        self.kinds = [kind for kind, _, _ in plan]
        self.widths = [width for _, width, _ in plan]
        self.ways = [ways for _, _, ways in plan]
        self.count = len(plan)
        self.sent = []

    def columns(self, c):
        return pl.ds(sum(self.widths[:c]), self.widths[c])

    def finish(self):
        for copy in self.sent:
            copy.wait_send()


class Gather(Plan):
    def __init__(self, plan, buf, send_sem, recv_sem):
        super().__init__(plan)
        self.buf, self.send_sem, self.recv_sem = buf, send_sem, recv_sem

    def copy(self, c, dz, dt, slot, device):
        part = self.buf.at[rows_of(dz, dt), self.columns(c)]
        return pltpu.make_async_remote_copy(
            src_ref=part,
            dst_ref=part,
            send_sem=self.send_sem.at[c, slot],
            recv_sem=self.recv_sem.at[c, slot],
            device_id=device,
            device_id_type=MESH,
        )

    def run(self, steps, compute, side=None, prepare=None):
        ready, begun = set(), set()
        for kind, *step in steps:
            if kind == 0:
                c, dz, dt = step
                self.copy(c, dz, dt, dz * 2 + dt, neighbour(1, 0)).wait_recv()
            elif kind == 1:
                way, c, dz, dt = step
                from_z, from_t = (dz + way) % N_DP, dt if way else 1 - dt
                if (from_z, from_t) == (0, 0) and c not in ready:
                    ready.add(c)
                    if prepare is not None:
                        prepare(c)
                device = neighbour(way, 0) if way else neighbour(0, 1)
                copy = self.copy(c, from_z, from_t, dz * 2 + dt, device)
                copy.start()
                self.sent.append(copy)
            elif kind == 2:
                c, r = step
                compute(c, r, r not in begun)
                begun.add(r)
            else:
                side(step[0])


RING = ((1, 0), (-1, 0), (0, 1))


class Scatter(Plan):
    def __init__(self, plan, part, land, send_sem, recv_sem):
        super().__init__(plan)
        self.part, self.land = part, land
        self.send_sem, self.recv_sem = send_sem, recv_sem

    def view(self, dz, dt, c):
        return self.part.at[rows_of(dz, dt), self.columns(c)]

    def copy(self, c, dz, dt, slot, device):
        return pltpu.make_async_remote_copy(
            src_ref=self.view(dz, dt, c),
            dst_ref=self.land.at[slot, :, self.columns(c)],
            send_sem=self.send_sem.at[c, slot],
            recv_sem=self.recv_sem.at[c, slot],
            device_id=device,
            device_id_type=MESH,
        )

    def send(self, c, dz, dt, way, slot):
        device = neighbour(way, 0) if way else neighbour(0, 1)
        copy = self.copy(c, dz, dt, slot, device)
        copy.start()
        self.sent.append(copy)

    def block(self, c, slot):
        first, last = self.ways[c][0], self.ways[c][-1]
        if self.kinds[c] == "A":
            names = ((2, 0), (2, 1), (-first, 0), (-last, 1), (first, 0), (last, 1), (0, 1))
        else:
            names = ((2, 1), (first, 1), (-first, 1), (0, 1), (2, 0), (-first, 0), (first, 0))
        return names[slot]

    def run(self, steps, compute, done):
        for kind, c, *step in steps:
            if kind == 0:
                compute(c)
            elif kind == 1:
                way, slot = step
                self.send(c, *self.block(c, slot), way, slot)
            else:
                slots, way, slot = step
                dz, dt = (0, 0) if way is None else self.block(c, slot)
                rows = rows_of(dz, dt)
                total = self.part[rows, self.columns(c)].astype(f32)
                for came in slots:
                    self.copy(c, 0, 0, came, neighbour(1, 0)).wait_recv()
                    total = total + self.land[came, :, self.columns(c)].astype(f32)
                if way is None:
                    done(c, total)
                else:
                    self.part[rows, self.columns(c)] = total.astype(bf16)
                    self.send(c, dz, dt, way, slot)


def params(collective_id=None, limit=62 * 1024 * 1024):
    if collective_id is None:
        return pltpu.CompilerParams(vmem_limit_bytes=limit)
    return pltpu.CompilerParams(
        collective_id=collective_id, has_side_effects=True, vmem_limit_bytes=limit
    )


def ring_sems(plan):
    return [pltpu.SemaphoreType.DMA((len(plan), 8)), pltpu.SemaphoreType.DMA((len(plan), 8))]


def land_scratch():
    return [pltpu.VMEM((TOTAL, D), bf16), pltpu.VMEM((7, ROWS, D), bf16)]


def image_rows(i):
    return pl.ds(pl.multiple_of(i * PATCHES, PATCHES), PATCHES)


def project_chunk(buf, wbuf, proj, turned, first, cols, r):
    rows = pl.ds(r * PATCHES, PATCHES)
    block = buf[rows, cols]
    value = dot_nn(block, wbuf[cols, :])
    if first:
        proj[rows, :] = value
    else:
        proj[rows, :] += value
    turned[cols, rows] = block.T


def side_by_side(w_hbm, wbuf, sems):
    return [
        pltpu.make_async_copy(w_hbm.at[t], wbuf.at[:, pl.ds(t * F, F)], sems.at[t])
        for t in range(3)
    ]


def head_cols(t, h):
    return pl.ds(t * F + h * HS, HS)


def head_state(q, k, v, pair):
    q_normed, q_unit, q_inv = norm_last(q, pair[0:1, :])
    k_normed, k_unit, k_inv = norm_last(k, pair[1:2, :])
    q_half, k_half = q_normed.astype(bf16), k_normed.astype(bf16)
    v_half = v.astype(bf16)
    exponent = jnp.exp(dot_nt(q_half, k_half) * (1.0 / math.sqrt(HS)))
    probs = exponent * (1.0 / jnp.sum(exponent, axis=-1, keepdims=True))
    return q_unit, q_inv, k_unit, k_inv, q_half, k_half, v_half, probs


def state_of(proj, pair, rows, h):
    return head_state(*[proj[rows, head_cols(t, h)] for t in range(3)], pair)


def attend(proj, pair_ref, att, turned):
    def image(i, carry):
        rows = image_rows(i)
        for h in range(3):
            v_half, probs = state_of(proj, pair_ref[...], rows, h)[-2:]
            mixed = dot_nn(probs.astype(bf16), v_half)
            att[rows, pl.ds(h * HS, HS)] = mixed.astype(bf16)
            if turned is not None:
                turned[pl.ds(h * HS, HS), rows] = mixed.T.astype(bf16)
        return carry

    lax.fori_loop(0, 2, image, 0)


def keep_scratch():
    return [
        pltpu.VMEM((6, PATCHES, PATCHES), f32),
        pltpu.VMEM((6, PATCHES, PATCHES), bf16),
        pltpu.VMEM((TOTAL, 3 * F), bf16),
        pltpu.VMEM((TOTAL, 2 * F), f32),
        pltpu.VMEM((12, PATCHES, 1), f32),
    ]


def keep_image(proj, pair_ref, kept, i, sums=None):
    probs_ref, turned_ref, halves_ref, unit_ref, inv_ref = kept
    rows = image_rows(i)
    for h in range(3):
        q_unit, q_inv, k_unit, k_inv, q_half, k_half, v_half, probs = state_of(
            proj, pair_ref[...], rows, h
        )
        slot = i * 3 + h
        probs_ref[slot] = probs
        turned_ref[slot] = probs.T.astype(bf16)
        for t, value in enumerate((q_half, k_half, v_half)):
            halves_ref[rows, head_cols(t, h)] = value
        unit_ref[rows, head_cols(0, h)] = q_unit
        unit_ref[rows, head_cols(1, h)] = k_unit
        inv_ref[2 * slot] = q_inv
        inv_ref[2 * slot + 1] = k_inv
        if sums is not None:
            mixed = dot_nn(probs.astype(bf16), v_half).astype(bf16).astype(f32)
            row_id = lax.broadcasted_iota(jnp.int32, (8, 1), 0)
            total = jnp.sum(mixed, axis=0, keepdims=True)
            sums[:, pl.ds(h * HS, HS)] += jnp.where(row_id == i, total, 0.0)


def back_image(kept, pair_ref, mixed_of, out, i):
    probs_ref, turned_ref, halves_ref, unit_ref, inv_ref = kept
    rows = image_rows(i)
    pair = pair_ref[...]
    for h in range(3):
        slot = i * 3 + h
        probs = probs_ref[slot]
        q_half, k_half, v_half = [halves_ref[rows, head_cols(t, h)] for t in range(3)]
        mixed = mixed_of(i, rows, h)
        grad_probs = dot_nt(mixed, v_half)
        grad_value = dot_nn(turned_ref[slot], mixed)
        grad_scores = probs * (grad_probs - jnp.sum(probs * grad_probs, axis=-1, keepdims=True))
        scaled = grad_scores * (1.0 / math.sqrt(HS))
        grad_query = dot_nn(scaled.astype(bf16), k_half)
        grad_key = dot_nn(scaled.T.astype(bf16), q_half)
        q_unit, k_unit = [unit_ref[rows, head_cols(t, h)] for t in range(2)]
        back_q = norm_back(grad_query, q_unit, inv_ref[2 * slot], pair[0:1, :])
        back_k = norm_back(grad_key, k_unit, inv_ref[2 * slot + 1], pair[1:2, :])
        for t, value in enumerate((back_q, back_k, grad_value)):
            out[rows, head_cols(t, h)] = value.astype(bf16)


def both_images(step):
    def body(i, carry):
        step(i)
        return carry

    lax.fori_loop(0, 2, body, 0)


PEERS = tuple((dz, dt) for dz in range(N_DP) for dt in range(N_T) if dz or dt)
PACK = D // 4


def front_kernel(
    rows_ref,
    gain_ref,
    pair_ref,
    pool_ref,
    label_ref,
    w_hbm,
    wout_hbm,
    head_hbm,
    out_ref,
    margin_ref,
    proj_hbm,
    turned_hbm,
    att_turned_ref,
    margin_turned_hbm,
    margin_grad_ref,
    head_grad_ref,
    image_ref,
    sums_ref,
    loss_ref,
    wbuf,
    wout,
    head,
    buf_own,
    buf_margin,
    proj_own,
    proj_margin,
    turned_own,
    turned_margin,
    att,
    part,
    land,
    next_rows,
    stage,
    pool_land,
    pooled_ref,
    half_ref,
    per_image,
    *rest,
):
    kept = rest[:5]
    (
    load_sem,
    store_sem,
    own_send,
    own_recv,
    sum_send,
    sum_recv,
    step_send,
    step_recv,
    margin_send,
    margin_recv,
    pool_send,
    pool_recv,
    ) = rest[5:]
    load_w = side_by_side(w_hbm, wbuf, load_sem)
    load_out = pltpu.make_async_copy(wout_hbm, wout, load_sem.at[3])
    load_head = pltpu.make_async_copy(head_hbm, head, load_sem.at[4])
    for load in load_w:
        load.start()
    load_out.start()
    load_head.start()
    devices = [neighbour(*way) for way in PEERS] + [section_at(1), section_at(-1)]
    greet(devices)
    normed, _, _ = norm_last(rows_ref[...].astype(f32), gain_ref[...])
    buf_own[rows_of(0, 0), :] = normed.astype(bf16)
    enter(devices)

    gather = Gather(PROJECT_PLAN, buf_own, own_send, own_recv)

    waiting = list(load_w)

    def compute_own(c, r, first):
        while waiting:
            waiting.pop().wait()
        project_chunk(buf_own, wbuf, proj_own, turned_own, first, gather.columns(c), r)

    gather.run(PROJECT_STEPS, compute_own)
    stores = [
        pltpu.make_async_copy(proj_own, proj_hbm, store_sem.at[0]),
        pltpu.make_async_copy(turned_own, turned_hbm, store_sem.at[1]),
    ]
    for store in stores:
        store.start()
    attend(proj_own, pair_ref, att, att_turned_ref)

    load_out.wait()
    scatter = Scatter(OUT_PLAN, part, land, sum_send, sum_recv)
    hops = []

    def out_chunk(c):
        cols = scatter.columns(c)

        def tile(r, carry):
            rows = image_rows(r)
            part[rows, cols] = dot_nn(att[rows, :], wout[:, cols]).astype(bf16)
            return carry

        lax.fori_loop(0, TOTAL // PATCHES, tile, 0)

    def out_done(c, total):
        cols = scatter.columns(c)
        out_ref[:, cols] = (rows_ref[:, cols].astype(f32) + total).astype(bf16)
        copy = pltpu.make_async_remote_copy(
            src_ref=out_ref.at[:, cols],
            dst_ref=next_rows.at[:, cols],
            send_sem=step_send.at[c],
            recv_sem=step_recv.at[c],
            device_id=section_at(1),
            device_id_type=MESH,
        )
        copy.start()
        hops.append(copy)

    scatter.run(OUT_STEPS, out_chunk, out_done)
    for copy in hops:
        copy.wait_recv()
    first = lax.axis_index("section") == 0
    margin = jnp.where(first, rows_ref[...], next_rows[...])
    margin_ref[...] = margin
    normed, _, _ = norm_last(margin.astype(f32), gain_ref[...])
    buf_margin[rows_of(0, 0), :] = normed.astype(bf16)
    second = Gather(PROJECT_PLAN, buf_margin, margin_send, margin_recv)
    second.run(
        PROJECT_STEPS,
        lambda c, r, first: project_chunk(
            buf_margin, wbuf, proj_margin, turned_margin, first, second.columns(c), r
        ),
    )
    store = pltpu.make_async_copy(turned_margin, margin_turned_hbm, store_sem.at[2])
    store.start()
    stores.append(store)
    sums_ref[...] = jnp.zeros_like(sums_ref)
    both_images(lambda i: keep_image(proj_margin, pair_ref, kept, i, sums_ref))

    row_id = lax.broadcasted_iota(jnp.int32, (8, 1), 0)
    sums = sums_ref[...]
    hi = sums.astype(bf16).astype(f32)
    mid = (sums - hi).astype(bf16).astype(f32)
    low = sums - hi - mid
    tall = jnp.concatenate([hi, mid, low], axis=0).astype(bf16)
    terms = dot_nn(tall, wout[...])
    partial_rows = terms[0:8] + terms[8:16] + terms[16:24]
    own = jnp.sum(margin_ref[...].astype(f32), axis=0, keepdims=True)
    image = lax.axis_index("dp") // (N_DP // 2)
    partial_rows = partial_rows + jnp.where(row_id == image, own, 0.0)
    for i in range(2):
        for q in range(4):
            stage[i * 4 + q : i * 4 + q + 1, :] = partial_rows[i : i + 1, q * PACK : (q + 1) * PACK]
    copies = []
    for k, way in enumerate(PEERS):
        copy = pltpu.make_async_remote_copy(
            src_ref=stage,
            dst_ref=pool_land.at[k],
            send_sem=pool_send.at[k],
            recv_sem=pool_recv.at[k],
            device_id=neighbour(*way),
            device_id_type=MESH,
        )
        copy.start()
        copies.append(copy)
    load_head.wait()
    total = stage[...]
    for k, copy in enumerate(copies):
        copy.wait_recv()
        total = total + pool_land[k]
    pooled_ref[...] = jnp.zeros_like(pooled_ref)
    for i in range(2):
        for q in range(4):
            pooled_ref[i : i + 1, q * PACK : (q + 1) * PACK] = total[i * 4 + q : i * 4 + q + 1, :]
    gain = pool_ref[...]
    normed, unit_rows, inverse = norm_last(pooled_ref[...] / PATCHES, gain)
    half = normed.astype(bf16)
    half_ref[...] = half.astype(f32)
    logits = dot_nn(half, head[...])
    label = jnp.where(row_id == 0, label_ref[0:1, 0:1], label_ref[0:1, 1:2])
    targets = (label == lax.broadcasted_iota(jnp.int32, (8, CLASSES), 1)).astype(f32)
    soft = jnp.maximum(logits, 0.0) + jnp.log1p(jnp.exp(-jnp.abs(logits)))
    loss = jnp.mean(soft - targets * logits, axis=-1, keepdims=True)
    lane = lax.broadcasted_iota(jnp.int32, (8, 128), 1)
    loss_ref[...] = jnp.sum(jnp.where(row_id == lane, loss, 0.0), axis=0, keepdims=True)[:, 0:2]
    grad_logits = (jax.nn.sigmoid(logits) - targets) / 2
    grad_logits = jnp.where(row_id < 2, grad_logits, 0.0).astype(bf16)
    grad_pooled = norm_back(dot_nt(grad_logits, head[...]), unit_rows, inverse, gain)
    grad_image = grad_pooled / PATCHES
    image_ref[...] = jnp.where(row_id < 2, grad_image, 0.0)
    per_image[...] = dot_nt(grad_image.astype(bf16), wout[...])
    z, t = place()
    width = D // (N_DP * N_T)
    start = pl.multiple_of((z * N_T + t) * width, width)
    mine = half_ref[:, pl.ds(start, width)]
    head_grad_ref[...] = dot_nn(mine.T.astype(bf16), grad_logits).astype(bf16)

    def shared_cotangent(i, rows, h):
        cols = pl.ds(h * HS, HS)
        row = jnp.where(i == 0, per_image[0:1, cols], per_image[1:2, cols])
        return jnp.broadcast_to(row, (PATCHES, HS)).astype(bf16)

    both_images(lambda i: back_image(kept, pair_ref, shared_cotangent, margin_grad_ref, i))
    gather.finish()
    scatter.finish()
    second.finish()
    for copy in hops + copies:
        copy.wait_send()
    for store in stores:
        store.wait()


def front(rows, gain_row, gain_pair, pool_row, labels, qkv_local, out_local, head_local, collective_id):
    return pl.pallas_call(
        front_kernel,
        out_shape=(
            jax.ShapeDtypeStruct((ROWS, D), bf16),
            jax.ShapeDtypeStruct((ROWS, D), bf16),
            jax.ShapeDtypeStruct((TOTAL, 3 * F), f32),
            jax.ShapeDtypeStruct((D, TOTAL), bf16),
            jax.ShapeDtypeStruct((F, TOTAL), bf16),
            jax.ShapeDtypeStruct((D, TOTAL), bf16),
            jax.ShapeDtypeStruct((TOTAL, 3 * F), bf16),
            jax.ShapeDtypeStruct((F, CLASSES), bf16),
            jax.ShapeDtypeStruct((8, D), f32),
            jax.ShapeDtypeStruct((8, F), f32),
            jax.ShapeDtypeStruct((1, 2), f32),
        ),
        in_specs=[VM, VM, VM, VM, VM, ANY, ANY, ANY],
        out_specs=(VM, VM, ANY, ANY, VM, ANY, VM, VM, VM, VM, VM),
        scratch_shapes=[
            pltpu.VMEM((D, 3 * F), bf16),
            pltpu.VMEM((F, D), bf16),
            pltpu.VMEM((D, CLASSES), bf16),
            pltpu.VMEM((TOTAL, D), bf16),
            pltpu.VMEM((TOTAL, D), bf16),
            pltpu.VMEM((TOTAL, 3 * F), f32),
            pltpu.VMEM((TOTAL, 3 * F), f32),
            pltpu.VMEM((D, TOTAL), bf16),
            pltpu.VMEM((D, TOTAL), bf16),
            pltpu.VMEM((TOTAL, F), bf16),
        ]
        + land_scratch()
        + [
            pltpu.VMEM((ROWS, D), bf16),
            pltpu.VMEM((8, PACK), f32),
            pltpu.VMEM((len(PEERS), 8, PACK), f32),
            pltpu.VMEM((8, D), f32),
            pltpu.VMEM((8, D), f32),
            pltpu.VMEM((8, F), f32),
        ]
        + keep_scratch()
        + [
            pltpu.SemaphoreType.DMA((5,)),
            pltpu.SemaphoreType.DMA((3,)),
        ]
        + ring_sems(PROJECT_PLAN)
        + ring_sems(OUT_PLAN)
        + [pltpu.SemaphoreType.DMA((len(OUT_PLAN),))] * 2
        + ring_sems(PROJECT_PLAN)
        + [pltpu.SemaphoreType.DMA((len(PEERS),)), pltpu.SemaphoreType.DMA((len(PEERS),))],
        compiler_params=params(collective_id),
        name="front",
    )(rows, gain_row, gain_pair, pool_row, labels, qkv_local, out_local, head_local)


def back_kernel(
    grad_ref,
    rows_ref,
    gain_ref,
    pair_ref,
    image_ref,
    sums_ref,
    w_hbm,
    wout_hbm,
    turned_hbm,
    margin_turned_hbm,
    proj_hbm,
    own_grad_ref,
    grad_out_hbm,
    margin_part_hbm,
    part,
    land,
    wbuf,
    wout,
    turned,
    margin_turned,
    total_ref,
    mine,
    came,
    buf,
    grad_out,
    margin_part,
    proj,
    grad_att_ref,
    *rest,
):
    kept = rest[:5]
    (
    wsem,
    load_sem,
    out_sem,
    part_sem,
    sum_send,
    sum_recv,
    step_send,
    step_recv,
    own_send,
    own_recv,
    ) = rest[5:]
    devices = [neighbour(*way) for way in RING] + [section_at(1), section_at(-1)]
    greet(devices)
    scatter = Scatter(INPUT_PLAN, part, land, sum_send, sum_recv)
    loads = []
    for c in range(scatter.count):
        for t in range(3):
            load = pltpu.make_async_copy(
                w_hbm.at[t, scatter.columns(c), :],
                wbuf.at[scatter.columns(c), pl.ds(t * F, F)],
                wsem.at[3 * c + t],
            )
            load.start()
            loads.append(load)
    later = [
        pltpu.make_async_copy(margin_turned_hbm, margin_turned, load_sem.at[0]),
        pltpu.make_async_copy(wout_hbm, wout, load_sem.at[1]),
        pltpu.make_async_copy(turned_hbm, turned, load_sem.at[2]),
        pltpu.make_async_copy(proj_hbm, proj, load_sem.at[3]),
    ]
    for load in later:
        load.start()
    enter(devices)

    def compute(c):
        for load in loads[3 * c : 3 * c + 3]:
            load.wait()
        cols = scatter.columns(c)

        def tile(r, carry):
            rows = image_rows(r)
            part[rows, cols] = dot_nt(grad_ref[rows, :], wbuf[cols, :]).astype(bf16)
            return carry

        lax.fori_loop(0, TOTAL // PATCHES, tile, 0)

    def done(c, total):
        total_ref[:, scatter.columns(c)] = total

    scatter.run(INPUT_STEPS, compute, done)
    gain = gain_ref[...]
    _, unit_rows, inverse = norm_last(rows_ref[...].astype(f32), gain)
    image = lax.axis_index("dp") // (N_DP // 2)
    residual = jnp.where(image == 0, image_ref[0:1, :], image_ref[1:2, :])
    grad = residual + norm_back(total_ref[...], unit_rows, inverse, gain)
    mine[...] = grad.astype(bf16)
    gather = Gather(RETURN_PLAN, buf, own_send, own_recv)
    copies = []
    for c in range(gather.count):
        copy = pltpu.make_async_remote_copy(
            src_ref=mine.at[:, gather.columns(c)],
            dst_ref=came.at[:, gather.columns(c)],
            send_sem=step_send.at[c],
            recv_sem=step_recv.at[c],
            device_id=section_at(-1),
            device_id_type=MESH,
        )
        copy.start()
        copies.append(copy)
    for load in later:
        load.wait()
    last = lax.axis_index("section") == lax.axis_size("section") - 1

    def take_hop(c):
        copies[c].wait_recv()
        block = came[:, gather.columns(c)]
        buf[rows_of(0, 0), gather.columns(c)] = jnp.where(last, jnp.zeros_like(block), block)

    sums_t = sums_ref[...].T
    hi = sums_t.astype(bf16)
    low = (sums_t - hi.astype(f32)).astype(bf16)
    stores = []

    def margin_piece(k):
        def tile(r, carry):
            part_rows = pl.ds(pl.multiple_of(k * TALL + r * 256, 256), 256)
            margin_part[part_rows, :] = dot_nn(
                margin_turned[part_rows, :], grad_ref[...]
            ).astype(bf16)
            return carry

        lax.fori_loop(0, TALL // 256, tile, 0)
        rows = pl.ds(k * TALL, TALL)
        store = pltpu.make_async_copy(
            margin_part.at[rows, :], margin_part_hbm.at[rows, :], part_sem.at[k]
        )
        store.start()
        stores.append(store)

    def chunk(c, r, first):
        cols = gather.columns(c)
        rows = pl.ds(r * PATCHES, PATCHES)
        value = dot_nt(buf[rows, cols], wout[:, cols])
        if first:
            grad_att_ref[rows, :] = value
        else:
            grad_att_ref[rows, :] += value
        if r == 0:
            return
        shared = image_ref[:, cols].astype(bf16)
        value = dot_nn(turned[...], buf[:, cols])
        value = value + dot_nn(hi, shared) + dot_nn(low, shared)
        grad_out[:, cols] = value.astype(bf16)
        store = pltpu.make_async_copy(
            grad_out.at[:, cols], grad_out_hbm.at[:, cols], out_sem.at[c]
        )
        store.start()
        stores.append(store)

    def side(i):
        if i < 2:
            keep_image(proj, pair_ref, kept, i)
        else:
            margin_piece(i - 2)

    gather.run(RETURN_STEPS, chunk, side, take_hop)

    def cotangent(i, rows, h):
        return grad_att_ref[rows, pl.ds(h * HS, HS)].astype(bf16)

    both_images(lambda i: back_image(kept, pair_ref, cotangent, own_grad_ref, i))
    scatter.finish()
    gather.finish()
    for copy in copies:
        copy.wait_send()
    for store in stores:
        store.wait()


def back(
    grad,
    rows,
    gain_row,
    gain_pair,
    grad_image,
    sums,
    qkv_local,
    out_local,
    turned,
    margin_turned,
    projected,
    collective_id,
):
    return pl.pallas_call(
        back_kernel,
        out_shape=(
            jax.ShapeDtypeStruct((TOTAL, 3 * F), bf16),
            jax.ShapeDtypeStruct((F, D), bf16),
            jax.ShapeDtypeStruct((D, 3 * F), bf16),
        ),
        in_specs=[VM] * 6 + [ANY] * 5,
        out_specs=(VM, ANY, ANY),
        scratch_shapes=land_scratch()
        + [
            pltpu.VMEM((D, 3 * F), bf16),
            pltpu.VMEM((F, D), bf16),
            pltpu.VMEM((F, TOTAL), bf16),
            pltpu.VMEM((D, TOTAL), bf16),
            pltpu.VMEM((ROWS, D), f32),
            pltpu.VMEM((ROWS, D), bf16),
            pltpu.VMEM((ROWS, D), bf16),
            pltpu.VMEM((TOTAL, D), bf16),
            pltpu.VMEM((F, D), bf16),
            pltpu.VMEM((D, 3 * F), bf16),
            pltpu.VMEM((TOTAL, 3 * F), f32),
            pltpu.VMEM((TOTAL, F), f32),
        ]
        + keep_scratch()
        + [
            pltpu.SemaphoreType.DMA((3 * len(INPUT_PLAN),)),
            pltpu.SemaphoreType.DMA((4,)),
            pltpu.SemaphoreType.DMA((len(RETURN_PLAN),)),
            pltpu.SemaphoreType.DMA((STEPS,)),
        ]
        + ring_sems(INPUT_PLAN)
        + [pltpu.SemaphoreType.DMA((len(RETURN_PLAN),))] * 2
        + ring_sems(RETURN_PLAN),
        compiler_params=params(collective_id),
        name="back",
    )(
        grad,
        rows,
        gain_row,
        gain_pair,
        grad_image,
        sums,
        qkv_local,
        out_local,
        turned,
        margin_turned,
        projected,
    )


def finish_kernel(
    grad_ref,
    turned_hbm,
    part_hbm,
    out_in,
    grad_out_in,
    head_in,
    grad_hbm,
    out_hbm,
    grad_out_hbm,
    head_hbm,
    turned,
    part,
    result,
    passed_out,
    passed_grad,
    passed_head,
    load_sem,
    part_sem,
    store_sem,
    pass_sem,
):
    passes = [
        (out_in, passed_out, out_hbm),
        (grad_out_in, passed_grad, grad_out_hbm),
        (head_in, passed_head, head_hbm),
    ]
    def tall_rows(r):
        return pl.ds(pl.multiple_of(r * TALL, TALL), TALL)

    def load_pair(r):
        rows = tall_rows(r)
        return (
            pltpu.make_async_copy(turned_hbm.at[rows, :], turned.at[rows, :], load_sem.at[r]),
            pltpu.make_async_copy(part_hbm.at[rows, :], part.at[rows, :], part_sem.at[r]),
        )

    def store(r):
        rows = tall_rows(r)
        return pltpu.make_async_copy(
            result.at[:, rows, :], grad_hbm.at[:, rows, :], store_sem.at[r]
        )

    for r in range(STEPS):
        for load in load_pair(r):
            load.start()
    through = []
    for k, (source, held, _) in enumerate(passes):
        copy = pltpu.make_async_copy(source, held, pass_sem.at[k])
        copy.start()
        through.append(copy)

    def step(r, carry):
        rows = tall_rows(r)
        for load in load_pair(r):
            load.wait()
        value = dot_nn(turned[rows, :], grad_ref[...]) + part[rows, :].astype(f32)
        for t in range(3):
            result[t, rows, :] = value[:, t * F : (t + 1) * F].astype(bf16)
        store(r).start()
        return carry

    lax.fori_loop(0, STEPS // 2, step, 0)
    stores = []
    for k, (_, held, target) in enumerate(passes):
        through[k].wait()
        copy = pltpu.make_async_copy(held, target, pass_sem.at[k])
        copy.start()
        stores.append(copy)
    lax.fori_loop(STEPS // 2, STEPS, step, 0)
    for copy in stores:
        copy.wait()
    for r in range(STEPS):
        store(r).wait()


def finish(grad, turned, margin_part, out_own, grad_out, grad_head):
    return pl.pallas_call(
        finish_kernel,
        out_shape=(
            jax.ShapeDtypeStruct((3, D, F), bf16),
            jax.ShapeDtypeStruct((ROWS, D), bf16),
            jax.ShapeDtypeStruct((F, D), bf16),
            jax.ShapeDtypeStruct((F, CLASSES), bf16),
        ),
        in_specs=[VM] + [ANY] * 5,
        out_specs=(ANY,) * 4,
        scratch_shapes=[
            pltpu.VMEM((D, TOTAL), bf16),
            pltpu.VMEM((D, 3 * F), bf16),
            pltpu.VMEM((3, D, F), bf16),
            pltpu.VMEM((ROWS, D), bf16),
            pltpu.VMEM((F, D), bf16),
            pltpu.VMEM((F, CLASSES), bf16),
            pltpu.SemaphoreType.DMA((STEPS,)),
            pltpu.SemaphoreType.DMA((STEPS,)),
            pltpu.SemaphoreType.DMA((STEPS,)),
            pltpu.SemaphoreType.DMA((3,)),
        ],
        compiler_params=params(),
        name="finish",
    )(grad, turned, margin_part, out_own, grad_out, grad_head)


def on_device(
    block_inputs, qkv_weights, out_weights, norm_gain, query_key_gain, pool_gain, class_head, labels
):
    rows_in, qkv_local, out_local = block_inputs[0], qkv_weights[0], out_weights[0]
    gain_pair = query_key_gain[0]
    (
        out_own,
        margin_rows,
        projected,
        turned,
        attention_turned,
        margin_turned,
        margin_grad,
        grad_head,
        grad_image,
        sums,
        losses,
    ) = front(
        rows_in, norm_gain, gain_pair, pool_gain, labels, qkv_local, out_local, class_head[0], 0
    )
    own_grad, grad_out, margin_part = back(
        margin_grad,
        margin_rows,
        norm_gain,
        gain_pair,
        grad_image,
        sums,
        qkv_local,
        out_local,
        attention_turned,
        margin_turned,
        projected,
        1,
    )
    qkv_grad, out_own, grad_out, grad_head = finish(
        own_grad, turned, margin_part, out_own, grad_out, grad_head
    )
    return (out_own[None], qkv_grad[None], grad_out[None], grad_head[None], losses)


def solution(mesh):
    in_specs = (
        P("section", ("dp", "tensor"), None),
        P("section", None, None, ("dp", "tensor")),
        P("section", ("dp", "tensor"), None),
        P("section", None),
        P("section", None, None),
        P("section", None),
        P("section", None, None),
        P("section", None),
    )
    out_specs = (
        P("section", ("dp", "tensor"), None),
        P("section", None, None, ("dp", "tensor")),
        P("section", ("dp", "tensor"), None),
        P("section", ("dp", "tensor"), None),
        P("section", None),
    )
    return jax.shard_map(
        on_device, mesh=mesh, in_specs=in_specs, out_specs=out_specs, check_vma=False
    )
```

```python
import functools
import math

import jax
import jax.numpy as jnp
from jax import lax
from jax.experimental import pallas as pl
from jax.experimental.pallas import tpu as pltpu
from jax.sharding import PartitionSpec as P

HS = 128
PATCHES = 256
EPS = 1e-06
N_DP = 4
N_T = 2
ROWS = 64
TOTAL = 512
D = 3072
F = 384
TALL = 512
STEPS = D // TALL
CLASSES = 512
PROJECT_PLAN = (('A', 768, (1, 1)), ('B', 1024, (-1,)), ('A', 256, (1, -1)), ('B', 256, (-1,)), ('B', 256, (1,)), ('A', 512, (-1, -1)))
PROJECT_STEPS = (
    (1, 0, 0, 0, 1), (1, 1, 0, 3, 0), (1, -1, 0, 1, 0), (1, 0, 1, 0, 1), (1, 1, 1, 3, 0), (1, -1, 1, 1, 0),
    (0, 0, 3, 0), (1, 1, 0, 2, 0), (0, 0, 1, 0), (1, 0, 2, 0, 1), (1, -1, 2, 1, 0), (0, 0, 0, 1),
    (1, 1, 0, 3, 1), (1, -1, 0, 1, 1), (1, 0, 3, 0, 1), (1, 0, 4, 0, 1), (1, 0, 5, 0, 1), (0, 1, 3, 0),
    (1, 0, 1, 3, 1), (0, 1, 1, 0), (1, -1, 1, 2, 0), (1, 0, 1, 1, 1), (0, 2, 1, 0), (0, 1, 0, 1),
    (0, 2, 0, 1), (1, 1, 2, 3, 1), (1, -1, 2, 1, 1), (0, 0, 2, 0), (0, 3, 0, 1), (1, 1, 2, 3, 0),
    (0, 0, 1, 1), (0, 4, 0, 1), (1, 1, 3, 3, 0), (1, 1, 4, 3, 0), (1, -1, 3, 1, 0), (0, 0, 3, 1),
    (1, 1, 0, 2, 1), (0, 5, 0, 1), (1, 1, 5, 3, 1), (1, -1, 5, 1, 1), (0, 2, 3, 1), (0, 2, 3, 0),
    (1, 1, 2, 2, 0), (0, 1, 2, 0), (1, 0, 1, 2, 1), (1, -1, 4, 1, 0), (0, 3, 3, 0), (1, 0, 3, 3, 1),
    (0, 2, 1, 1), (1, -1, 2, 2, 1), (0, 4, 3, 0), (1, 1, 4, 2, 0), (1, 0, 4, 3, 1), (0, 3, 1, 0),
    (1, -1, 3, 2, 0), (1, 0, 3, 1, 1), (0, 1, 3, 1), (1, -1, 5, 1, 0), (0, 5, 1, 1), (1, -1, 5, 2, 1),
    (0, 0, 2, 1), (2, 0, 0), (0, 4, 1, 0), (1, 0, 4, 1, 1), (0, 2, 2, 1), (0, 1, 1, 1),
    (1, 1, 5, 3, 0), (2, 0, 1), (0, 5, 3, 1), (0, 3, 2, 0), (1, 0, 3, 2, 1), (0, 2, 2, 0),
    (2, 2, 0), (2, 2, 1), (0, 4, 2, 0), (1, 0, 4, 2, 1), (0, 5, 1, 0), (1, -1, 5, 2, 0),
    (0, 1, 2, 1), (2, 1, 0), (0, 5, 3, 0), (0, 5, 2, 1), (0, 3, 3, 1), (2, 1, 1),
    (0, 4, 3, 1), (0, 3, 1, 1), (0, 5, 2, 0), (2, 5, 0), (0, 4, 1, 1), (2, 5, 1),
    (0, 3, 2, 1), (2, 3, 0), (2, 3, 1), (0, 4, 2, 1), (2, 4, 0), (2, 4, 1),
)
RETURN_PLAN = (('B', 256, (-1,)), ('B', 256, (1,)), ('A', 1024, (-1, 1)), ('B', 256, (-1,)), ('A', 768, (-1, 1)), ('B', 512, (1,)))
RETURN_STEPS = (
    (1, 1, 0, 3, 0), (1, -1, 0, 1, 0), (1, 0, 0, 0, 1), (1, 1, 1, 3, 0), (1, -1, 1, 1, 0), (1, 0, 1, 0, 1),
    (1, 0, 2, 0, 1), (1, 1, 2, 3, 0), (1, -1, 2, 1, 0), (1, 1, 3, 3, 0), (1, -1, 3, 1, 0), (1, 0, 3, 0, 1),
    (1, 0, 4, 0, 1), (1, 1, 4, 3, 0), (1, -1, 4, 1, 0), (3, 0), (3, 1), (0, 0, 3, 0),
    (1, 0, 0, 3, 1), (0, 0, 1, 0), (1, -1, 0, 2, 0), (1, 0, 0, 1, 1), (1, 1, 5, 3, 0), (1, -1, 5, 1, 0),
    (3, 2), (0, 1, 3, 0), (1, 1, 1, 2, 0), (1, 0, 1, 3, 1), (0, 1, 1, 0), (1, 0, 1, 1, 1),
    (0, 0, 0, 1), (3, 3), (0, 1, 0, 1), (3, 4), (1, 0, 5, 0, 1), (3, 5),
    (0, 2, 3, 0), (0, 2, 1, 0), (1, -1, 2, 2, 0), (3, 6), (0, 3, 3, 0), (1, 0, 3, 3, 1),
    (0, 3, 1, 0), (1, -1, 3, 2, 0), (1, 0, 3, 1, 1), (0, 2, 0, 1), (1, 1, 2, 3, 1), (1, -1, 2, 1, 1),
    (3, 7), (0, 3, 0, 1), (0, 4, 3, 0), (0, 4, 1, 0), (1, -1, 4, 2, 0), (0, 0, 2, 0),
    (1, 0, 0, 2, 1), (0, 4, 0, 1), (1, 1, 4, 3, 1), (1, -1, 4, 1, 1), (0, 5, 3, 0), (1, 1, 5, 2, 0),
    (1, 0, 5, 3, 1), (0, 0, 3, 1), (0, 1, 2, 0), (1, 0, 1, 2, 1), (0, 5, 1, 0), (1, 0, 5, 1, 1),
    (0, 0, 1, 1), (0, 1, 3, 1), (0, 1, 1, 1), (0, 2, 3, 1), (1, 1, 2, 2, 1), (0, 2, 2, 0),
    (0, 5, 0, 1), (0, 3, 2, 0), (1, 0, 3, 2, 1), (0, 3, 3, 1), (0, 3, 1, 1), (0, 4, 3, 1),
    (1, 1, 4, 2, 1), (0, 0, 2, 1), (2, 0, 0), (2, 0, 1), (0, 5, 2, 0), (1, 0, 5, 2, 1),
    (0, 2, 1, 1), (0, 5, 3, 1), (0, 1, 2, 1), (2, 1, 0), (2, 1, 1), (0, 4, 2, 0),
    (0, 5, 1, 1), (0, 2, 2, 1), (2, 2, 0), (0, 3, 2, 1), (2, 2, 1), (2, 3, 0),
    (0, 4, 1, 1), (2, 3, 1), (0, 5, 2, 1), (2, 5, 0), (2, 5, 1), (0, 4, 2, 1),
    (2, 4, 0), (2, 4, 1),
)
OUT_PLAN = (('A', 512, (1, 1)), ('A', 256, (1, 1)), ('B', 1280, (-1,)), ('A', 512, (-1, 1)), ('A', 512, (1, -1)))
OUT_STEPS = (
    (0, 0), (1, 0, 1, 0), (1, 0, 1, 1), (1, 0, -1, 2), (1, 0, -1, 3), (0, 1),
    (0, 2), (1, 2, 0, 0), (0, 3), (1, 1, 1, 0), (1, 1, -1, 2), (0, 4),
    (1, 1, 1, 1), (1, 1, -1, 3), (1, 3, 1, 1), (1, 2, 0, 1), (1, 3, -1, 0), (2, 0, (0,), 1, 4),
    (1, 3, -1, 3), (2, 0, (1,), 1, 5), (1, 4, -1, 1), (2, 1, (0,), 1, 4), (1, 2, 0, 2), (2, 1, (1,), 1, 5),
    (1, 4, -1, 2), (2, 2, (0,), -1, 4), (2, 3, (1,), 1, 5), (2, 3, (0,), -1, 4), (1, 3, 1, 2), (1, 2, 0, 3),
    (2, 0, (3, 5), 0, 6), (2, 4, (1,), -1, 5), (1, 4, 1, 0), (2, 1, (3, 5), 0, 6), (1, 4, 1, 3), (2, 3, (3, 5), 0, 6),
    (2, 2, (2,), 1, 5), (2, 2, (1, 4), -1, 6), (2, 4, (0,), 1, 4), (2, 4, (3, 5), 0, 6), (2, 0, (2, 4, 6), None, None), (2, 1, (2, 4, 6), None, None),
    (2, 3, (2, 4, 6), None, None), (2, 2, (3, 5, 6), None, None), (2, 4, (2, 4, 6), None, None),
)
INPUT_PLAN = (('B', 256, (-1,)), ('A', 768, (-1, 1)), ('B', 256, (1,)), ('B', 1024, (1,)), ('A', 512, (1, -1)), ('A', 256, (-1, -1)))
INPUT_STEPS = (
    (0, 0), (1, 0, 0, 0), (1, 0, 0, 1), (1, 0, 0, 2), (1, 0, 0, 3), (0, 1),
    (1, 1, -1, 0), (1, 1, 1, 1), (1, 1, 1, 2), (1, 1, -1, 3), (0, 2), (1, 2, 0, 0),
    (1, 2, 0, 1), (1, 2, 0, 2), (1, 2, 0, 3), (0, 3), (2, 0, (0,), -1, 4), (2, 0, (2,), 1, 5),
    (1, 3, 0, 0), (1, 3, 0, 1), (1, 3, 0, 2), (1, 3, 0, 3), (0, 4), (2, 1, (0,), -1, 4),
    (2, 1, (1,), 1, 5), (2, 2, (0,), 1, 4), (1, 4, 1, 0), (1, 4, -1, 1), (1, 4, -1, 2), (1, 4, 1, 3),
    (0, 5), (2, 2, (2,), -1, 5), (1, 5, -1, 0), (1, 5, -1, 1), (1, 5, 1, 2), (1, 5, 1, 3),
    (2, 0, (1, 4), -1, 6), (2, 3, (0,), 1, 4), (2, 1, (3, 5), 0, 6), (2, 2, (1, 4), 1, 6), (2, 4, (1,), -1, 5), (2, 4, (0,), 1, 4),
    (2, 5, (0,), -1, 4), (2, 5, (1,), -1, 5), (2, 0, (3, 5, 6), None, None), (2, 3, (2,), -1, 5), (2, 4, (3, 5), 0, 6), (2, 3, (1, 4), 1, 6),
    (2, 5, (3, 5), 0, 6), (2, 2, (3, 5, 6), None, None), (2, 1, (2, 4, 6), None, None), (2, 4, (2, 4, 6), None, None), (2, 5, (2, 4, 6), None, None), (2, 3, (3, 5, 6), None, None),
)
MESH = pl.DeviceIdType.MESH
f32 = jnp.float32
bf16 = jnp.bfloat16
VM = pl.BlockSpec(memory_space=pltpu.VMEM)
ANY = pl.BlockSpec(memory_space=pl.ANY)


def dot_nn(a, b):
    return lax.dot_general(a, b, (((1,), (0,)), ((), ())), preferred_element_type=f32)


def dot_nt(a, b):
    return lax.dot_general(a, b, (((1,), (1,)), ((), ())), preferred_element_type=f32)


def norm_last(values, gain_row):
    centered = values - jnp.mean(values, axis=-1, keepdims=True)
    inverse = lax.rsqrt(jnp.mean(centered * centered, axis=-1, keepdims=True) + EPS)
    unit_rows = centered * inverse
    return unit_rows * gain_row, unit_rows, inverse


def norm_back(grad, unit_rows, inverse, gain_row):
    scaled = grad * gain_row
    return inverse * (
        scaled
        - jnp.mean(scaled, axis=-1, keepdims=True)
        - unit_rows * jnp.mean(scaled * unit_rows, axis=-1, keepdims=True)
    )


def place():
    return lax.axis_index("dp"), lax.axis_index("tensor")


def neighbour(dz, dt):
    z, t = place()
    target = {}
    if dz:
        target["dp"] = lax.rem(z + dz + N_DP, N_DP)
    if dt:
        target["tensor"] = 1 - t
    return target


def section_at(step):
    s, n = lax.axis_index("section"), lax.axis_size("section")
    return {"section": lax.rem(s + step + n, n)}


def greet(devices):
    barrier = pltpu.get_barrier_semaphore()
    for device in devices:
        pl.semaphore_signal(barrier, inc=1, device_id=device, device_id_type=MESH)


def enter(devices):
    pl.semaphore_wait(pltpu.get_barrier_semaphore(), len(devices))


def rows_of(dz, dt):
    z, t = place()
    owner = lax.rem(z + dz + N_DP, N_DP) * N_T + ((1 - t) if dt else t)
    return pl.ds(pl.multiple_of(owner * ROWS, ROWS), ROWS)


class Plan:
    def __init__(self, plan):
        self.kinds = [kind for kind, _, _ in plan]
        self.widths = [width for _, width, _ in plan]
        self.ways = [ways for _, _, ways in plan]
        self.count = len(plan)
        self.sent = []

    def columns(self, c):
        return pl.ds(sum(self.widths[:c]), self.widths[c])

    def finish(self):
        for copy in self.sent:
            copy.wait_send()


class Gather(Plan):
    def __init__(self, plan, buf, send_sem, recv_sem):
        super().__init__(plan)
        self.buf, self.send_sem, self.recv_sem = buf, send_sem, recv_sem

    def copy(self, c, dz, dt, slot, device):
        part = self.buf.at[rows_of(dz, dt), self.columns(c)]
        return pltpu.make_async_remote_copy(
            src_ref=part,
            dst_ref=part,
            send_sem=self.send_sem.at[c, slot],
            recv_sem=self.recv_sem.at[c, slot],
            device_id=device,
            device_id_type=MESH,
        )

    def run(self, steps, compute, side=None, prepare=None):
        ready, begun = set(), set()
        for kind, *step in steps:
            if kind == 0:
                c, dz, dt = step
                self.copy(c, dz, dt, dz * 2 + dt, neighbour(1, 0)).wait_recv()
            elif kind == 1:
                way, c, dz, dt = step
                from_z, from_t = (dz + way) % N_DP, dt if way else 1 - dt
                if (from_z, from_t) == (0, 0) and c not in ready:
                    ready.add(c)
                    if prepare is not None:
                        prepare(c)
                device = neighbour(way, 0) if way else neighbour(0, 1)
                copy = self.copy(c, from_z, from_t, dz * 2 + dt, device)
                copy.start()
                self.sent.append(copy)
            elif kind == 2:
                c, r = step
                compute(c, r, r not in begun)
                begun.add(r)
            else:
                side(step[0])


RING = ((1, 0), (-1, 0), (0, 1))


class Scatter(Plan):
    def __init__(self, plan, part, land, send_sem, recv_sem):
        super().__init__(plan)
        self.part, self.land = part, land
        self.send_sem, self.recv_sem = send_sem, recv_sem

    def view(self, dz, dt, c):
        return self.part.at[rows_of(dz, dt), self.columns(c)]

    def copy(self, c, dz, dt, slot, device):
        return pltpu.make_async_remote_copy(
            src_ref=self.view(dz, dt, c),
            dst_ref=self.land.at[slot, :, self.columns(c)],
            send_sem=self.send_sem.at[c, slot],
            recv_sem=self.recv_sem.at[c, slot],
            device_id=device,
            device_id_type=MESH,
        )

    def send(self, c, dz, dt, way, slot):
        device = neighbour(way, 0) if way else neighbour(0, 1)
        copy = self.copy(c, dz, dt, slot, device)
        copy.start()
        self.sent.append(copy)

    def block(self, c, slot):
        first, last = self.ways[c][0], self.ways[c][-1]
        if self.kinds[c] == "A":
            names = ((2, 0), (2, 1), (-first, 0), (-last, 1), (first, 0), (last, 1), (0, 1))
        else:
            names = ((2, 1), (first, 1), (-first, 1), (0, 1), (2, 0), (-first, 0), (first, 0))
        return names[slot]

    def run(self, steps, compute, done):
        for kind, c, *step in steps:
            if kind == 0:
                compute(c)
            elif kind == 1:
                way, slot = step
                self.send(c, *self.block(c, slot), way, slot)
            else:
                slots, way, slot = step
                dz, dt = (0, 0) if way is None else self.block(c, slot)
                rows = rows_of(dz, dt)
                total = self.part[rows, self.columns(c)].astype(f32)
                for came in slots:
                    self.copy(c, 0, 0, came, neighbour(1, 0)).wait_recv()
                    total = total + self.land[came, :, self.columns(c)].astype(f32)
                if way is None:
                    done(c, total)
                else:
                    self.part[rows, self.columns(c)] = total.astype(bf16)
                    self.send(c, dz, dt, way, slot)


def params(collective_id=None, limit=62 * 1024 * 1024):
    if collective_id is None:
        return pltpu.CompilerParams(vmem_limit_bytes=limit)
    return pltpu.CompilerParams(
        collective_id=collective_id, has_side_effects=True, vmem_limit_bytes=limit
    )


def ring_sems(plan):
    return [pltpu.SemaphoreType.DMA((len(plan), 8)), pltpu.SemaphoreType.DMA((len(plan), 8))]


def land_scratch():
    return [pltpu.VMEM((TOTAL, D), bf16), pltpu.VMEM((7, ROWS, D), bf16)]


def image_rows(i):
    return pl.ds(pl.multiple_of(i * PATCHES, PATCHES), PATCHES)


def project_chunk(buf, wbuf, proj, turned, first, cols, r):
    rows = pl.ds(r * PATCHES, PATCHES)
    block = buf[rows, cols]
    value = dot_nn(block, wbuf[cols, :])
    if first:
        proj[rows, :] = value
    else:
        proj[rows, :] += value
    turned[cols, rows] = block.T


def side_by_side(w_hbm, wbuf, sems):
    return [
        pltpu.make_async_copy(w_hbm.at[t], wbuf.at[:, pl.ds(t * F, F)], sems.at[t])
        for t in range(3)
    ]


def head_cols(t, h):
    return pl.ds(t * F + h * HS, HS)


def head_state(q, k, v, pair):
    q_normed, q_unit, q_inv = norm_last(q, pair[0:1, :])
    k_normed, k_unit, k_inv = norm_last(k, pair[1:2, :])
    q_half, k_half = q_normed.astype(bf16), k_normed.astype(bf16)
    v_half = v.astype(bf16)
    exponent = jnp.exp(dot_nt(q_half, k_half) * (1.0 / math.sqrt(HS)))
    probs = exponent * (1.0 / jnp.sum(exponent, axis=-1, keepdims=True))
    return q_unit, q_inv, k_unit, k_inv, q_half, k_half, v_half, probs


def state_of(proj, pair, rows, h):
    return head_state(*[proj[rows, head_cols(t, h)] for t in range(3)], pair)


def attend(proj, pair_ref, att, turned):
    def image(i, carry):
        rows = image_rows(i)
        for h in range(3):
            v_half, probs = state_of(proj, pair_ref[...], rows, h)[-2:]
            mixed = dot_nn(probs.astype(bf16), v_half)
            att[rows, pl.ds(h * HS, HS)] = mixed.astype(bf16)
            if turned is not None:
                turned[pl.ds(h * HS, HS), rows] = mixed.T.astype(bf16)
        return carry

    lax.fori_loop(0, 2, image, 0)


def keep_scratch():
    return [
        pltpu.VMEM((6, PATCHES, PATCHES), f32),
        pltpu.VMEM((6, PATCHES, PATCHES), bf16),
        pltpu.VMEM((TOTAL, 3 * F), bf16),
        pltpu.VMEM((TOTAL, 2 * F), f32),
        pltpu.VMEM((12, PATCHES, 1), f32),
    ]


def keep_image(proj, pair_ref, kept, i, sums=None):
    probs_ref, turned_ref, halves_ref, unit_ref, inv_ref = kept
    rows = image_rows(i)
    for h in range(3):
        q_unit, q_inv, k_unit, k_inv, q_half, k_half, v_half, probs = state_of(
            proj, pair_ref[...], rows, h
        )
        slot = i * 3 + h
        probs_ref[slot] = probs
        turned_ref[slot] = probs.T.astype(bf16)
        for t, value in enumerate((q_half, k_half, v_half)):
            halves_ref[rows, head_cols(t, h)] = value
        unit_ref[rows, head_cols(0, h)] = q_unit
        unit_ref[rows, head_cols(1, h)] = k_unit
        inv_ref[2 * slot] = q_inv
        inv_ref[2 * slot + 1] = k_inv
        if sums is not None:
            mixed = dot_nn(probs.astype(bf16), v_half).astype(bf16).astype(f32)
            row_id = lax.broadcasted_iota(jnp.int32, (8, 1), 0)
            total = jnp.sum(mixed, axis=0, keepdims=True)
            sums[:, pl.ds(h * HS, HS)] += jnp.where(row_id == i, total, 0.0)


def back_image(kept, pair_ref, mixed_of, out, i):
    probs_ref, turned_ref, halves_ref, unit_ref, inv_ref = kept
    rows = image_rows(i)
    pair = pair_ref[...]
    for h in range(3):
        slot = i * 3 + h
        probs = probs_ref[slot]
        q_half, k_half, v_half = [halves_ref[rows, head_cols(t, h)] for t in range(3)]
        mixed = mixed_of(i, rows, h)
        grad_probs = dot_nt(mixed, v_half)
        grad_value = dot_nn(turned_ref[slot], mixed)
        grad_scores = probs * (grad_probs - jnp.sum(probs * grad_probs, axis=-1, keepdims=True))
        scaled = grad_scores * (1.0 / math.sqrt(HS))
        grad_query = dot_nn(scaled.astype(bf16), k_half)
        grad_key = dot_nn(scaled.T.astype(bf16), q_half)
        q_unit, k_unit = [unit_ref[rows, head_cols(t, h)] for t in range(2)]
        back_q = norm_back(grad_query, q_unit, inv_ref[2 * slot], pair[0:1, :])
        back_k = norm_back(grad_key, k_unit, inv_ref[2 * slot + 1], pair[1:2, :])
        for t, value in enumerate((back_q, back_k, grad_value)):
            out[rows, head_cols(t, h)] = value.astype(bf16)


def both_images(step):
    def body(i, carry):
        step(i)
        return carry

    lax.fori_loop(0, 2, body, 0)


PEERS = tuple((dz, dt) for dz in range(N_DP) for dt in range(N_T) if dz or dt)
PACK = D // 4


def chain_kernel(
    rows_ref,
    gain_ref,
    pair_ref,
    pool_ref,
    label_ref,
    w_hbm,
    wout_hbm,
    head_hbm,
    out_ref,
    turned_hbm,
    head_grad_ref,
    loss_ref,
    own_grad_ref,
    grad_out_hbm,
    margin_part_hbm,
    margin_ref,
    att_turned_ref,
    margin_grad_ref,
    image_ref,
    sums_ref,
    wbuf,
    wout,
    head,
    buf_own,
    buf_margin,
    buf,
    proj_own,
    proj_margin,
    turned_own,
    turned_margin,
    att,
    part,
    land,
    back_land,
    next_rows,
    stage,
    pool_land,
    pooled_ref,
    half_ref,
    per_image,
    total_ref,
    mine,
    came,
    grad_out,
    grad_att_ref,
    load_sem,
    store_sem,
    step_send,
    step_recv,
    pool_send,
    pool_recv,
    hop_send,
    hop_recv,
    out_sem,
    part_sem,
    *rest,
):
    kept = rest[:5]
    (
        own_send,
        own_recv,
        sum_send,
        sum_recv,
        margin_send,
        margin_recv,
        back_send,
        back_recv,
        return_send,
        return_recv,
    ) = rest[5:]
    load_w = side_by_side(w_hbm, wbuf, load_sem)
    load_out = pltpu.make_async_copy(wout_hbm, wout, load_sem.at[3])
    load_head = pltpu.make_async_copy(head_hbm, head, load_sem.at[4])
    for load in load_w:
        load.start()
    load_out.start()
    load_head.start()
    devices = [neighbour(*way) for way in PEERS] + [section_at(1), section_at(-1)]
    greet(devices)
    normed, _, _ = norm_last(rows_ref[...].astype(f32), gain_ref[...])
    buf_own[rows_of(0, 0), :] = normed.astype(bf16)
    enter(devices)

    gather = Gather(PROJECT_PLAN, buf_own, own_send, own_recv)

    waiting = list(load_w)

    def compute_own(c, r, first):
        while waiting:
            waiting.pop().wait()
        project_chunk(buf_own, wbuf, proj_own, turned_own, first, gather.columns(c), r)

    gather.run(PROJECT_STEPS, compute_own)
    stores = [
        pltpu.make_async_copy(turned_own, turned_hbm, store_sem.at[0]),
    ]
    for store in stores:
        store.start()
    attend(proj_own, pair_ref, att, att_turned_ref)

    load_out.wait()
    scatter = Scatter(OUT_PLAN, part, land, sum_send, sum_recv)
    hops = []

    def out_chunk(c):
        cols = scatter.columns(c)

        def tile(r, carry):
            rows = image_rows(r)
            part[rows, cols] = dot_nn(att[rows, :], wout[:, cols]).astype(bf16)
            return carry

        lax.fori_loop(0, TOTAL // PATCHES, tile, 0)

    def out_done(c, total):
        cols = scatter.columns(c)
        out_ref[:, cols] = (rows_ref[:, cols].astype(f32) + total).astype(bf16)
        copy = pltpu.make_async_remote_copy(
            src_ref=out_ref.at[:, cols],
            dst_ref=next_rows.at[:, cols],
            send_sem=step_send.at[c],
            recv_sem=step_recv.at[c],
            device_id=section_at(1),
            device_id_type=MESH,
        )
        copy.start()
        hops.append(copy)

    scatter.run(OUT_STEPS, out_chunk, out_done)
    for copy in hops:
        copy.wait_recv()
    first = lax.axis_index("section") == 0
    margin = jnp.where(first, rows_ref[...], next_rows[...])
    margin_ref[...] = margin
    normed, _, _ = norm_last(margin.astype(f32), gain_ref[...])
    buf_margin[rows_of(0, 0), :] = normed.astype(bf16)
    second = Gather(PROJECT_PLAN, buf_margin, margin_send, margin_recv)
    second.run(
        PROJECT_STEPS,
        lambda c, r, first: project_chunk(
            buf_margin, wbuf, proj_margin, turned_margin, first, second.columns(c), r
        ),
    )
    sums_ref[...] = jnp.zeros_like(sums_ref)
    both_images(lambda i: keep_image(proj_margin, pair_ref, kept, i, sums_ref))

    row_id = lax.broadcasted_iota(jnp.int32, (8, 1), 0)
    sums = sums_ref[...]
    hi = sums.astype(bf16).astype(f32)
    mid = (sums - hi).astype(bf16).astype(f32)
    low = sums - hi - mid
    tall = jnp.concatenate([hi, mid, low], axis=0).astype(bf16)
    terms = dot_nn(tall, wout[...])
    partial_rows = terms[0:8] + terms[8:16] + terms[16:24]
    own = jnp.sum(margin_ref[...].astype(f32), axis=0, keepdims=True)
    image = lax.axis_index("dp") // (N_DP // 2)
    partial_rows = partial_rows + jnp.where(row_id == image, own, 0.0)
    for i in range(2):
        for q in range(4):
            stage[i * 4 + q : i * 4 + q + 1, :] = partial_rows[i : i + 1, q * PACK : (q + 1) * PACK]
    copies = []
    for k, way in enumerate(PEERS):
        copy = pltpu.make_async_remote_copy(
            src_ref=stage,
            dst_ref=pool_land.at[k],
            send_sem=pool_send.at[k],
            recv_sem=pool_recv.at[k],
            device_id=neighbour(*way),
            device_id_type=MESH,
        )
        copy.start()
        copies.append(copy)
    load_head.wait()
    total = stage[...]
    for k, copy in enumerate(copies):
        copy.wait_recv()
        total = total + pool_land[k]
    pooled_ref[...] = jnp.zeros_like(pooled_ref)
    for i in range(2):
        for q in range(4):
            pooled_ref[i : i + 1, q * PACK : (q + 1) * PACK] = total[i * 4 + q : i * 4 + q + 1, :]
    gain = pool_ref[...]
    normed, unit_rows, inverse = norm_last(pooled_ref[...] / PATCHES, gain)
    half = normed.astype(bf16)
    half_ref[...] = half.astype(f32)
    logits = dot_nn(half, head[...])
    label = jnp.where(row_id == 0, label_ref[0:1, 0:1], label_ref[0:1, 1:2])
    targets = (label == lax.broadcasted_iota(jnp.int32, (8, CLASSES), 1)).astype(f32)
    soft = jnp.maximum(logits, 0.0) + jnp.log1p(jnp.exp(-jnp.abs(logits)))
    loss = jnp.mean(soft - targets * logits, axis=-1, keepdims=True)
    lane = lax.broadcasted_iota(jnp.int32, (8, 128), 1)
    loss_ref[...] = jnp.sum(jnp.where(row_id == lane, loss, 0.0), axis=0, keepdims=True)[:, 0:2]
    grad_logits = (jax.nn.sigmoid(logits) - targets) / 2
    grad_logits = jnp.where(row_id < 2, grad_logits, 0.0).astype(bf16)
    grad_pooled = norm_back(dot_nt(grad_logits, head[...]), unit_rows, inverse, gain)
    grad_image = grad_pooled / PATCHES
    image_ref[...] = jnp.where(row_id < 2, grad_image, 0.0)
    per_image[...] = dot_nt(grad_image.astype(bf16), wout[...])
    z, t = place()
    width = D // (N_DP * N_T)
    start = pl.multiple_of((z * N_T + t) * width, width)
    pooled_slice = half_ref[:, pl.ds(start, width)]
    head_grad_ref[...] = dot_nn(pooled_slice.T.astype(bf16), grad_logits).astype(bf16)

    def shared_cotangent(i, rows, h):
        cols = pl.ds(h * HS, HS)
        row = jnp.where(i == 0, per_image[0:1, cols], per_image[1:2, cols])
        return jnp.broadcast_to(row, (PATCHES, HS)).astype(bf16)

    both_images(lambda i: back_image(kept, pair_ref, shared_cotangent, margin_grad_ref, i))
    gather.finish()
    scatter.finish()
    second.finish()
    for copy in hops + copies:
        copy.wait_send()
    for store in stores:
        store.wait()

    scatter = Scatter(INPUT_PLAN, part, back_land, back_send, back_recv)
    def compute(c):
        cols = scatter.columns(c)

        def tile(r, carry):
            rows = image_rows(r)
            part[rows, cols] = dot_nt(margin_grad_ref[rows, :], wbuf[cols, :]).astype(bf16)
            return carry

        lax.fori_loop(0, TOTAL // PATCHES, tile, 0)

    def done(c, total):
        total_ref[:, scatter.columns(c)] = total

    scatter.run(INPUT_STEPS, compute, done)
    gain = gain_ref[...]
    _, unit_rows, inverse = norm_last(margin_ref[...].astype(f32), gain)
    image = lax.axis_index("dp") // (N_DP // 2)
    residual = jnp.where(image == 0, image_ref[0:1, :], image_ref[1:2, :])
    grad = residual + norm_back(total_ref[...], unit_rows, inverse, gain)
    mine[...] = grad.astype(bf16)
    gather = Gather(RETURN_PLAN, buf, return_send, return_recv)
    copies = []
    for c in range(gather.count):
        copy = pltpu.make_async_remote_copy(
            src_ref=mine.at[:, gather.columns(c)],
            dst_ref=came.at[:, gather.columns(c)],
            send_sem=hop_send.at[c],
            recv_sem=hop_recv.at[c],
            device_id=section_at(-1),
            device_id_type=MESH,
        )
        copy.start()
        copies.append(copy)
    last = lax.axis_index("section") == lax.axis_size("section") - 1

    def take_hop(c):
        copies[c].wait_recv()
        block = came[:, gather.columns(c)]
        buf[rows_of(0, 0), gather.columns(c)] = jnp.where(last, jnp.zeros_like(block), block)

    sums_t = sums_ref[...].T
    hi = sums_t.astype(bf16)
    low = (sums_t - hi.astype(f32)).astype(bf16)
    stores = []

    def margin_piece(k):
        def tile(r, carry):
            part_rows = pl.ds(pl.multiple_of(k * TALL + r * 256, 256), 256)
            wbuf[part_rows, :] = dot_nn(
                turned_margin[part_rows, :], margin_grad_ref[...]
            ).astype(bf16)
            return carry

        lax.fori_loop(0, TALL // 256, tile, 0)
        rows = pl.ds(k * TALL, TALL)
        store = pltpu.make_async_copy(
            wbuf.at[rows, :], margin_part_hbm.at[rows, :], part_sem.at[k]
        )
        store.start()
        stores.append(store)

    def chunk(c, r, first):
        cols = gather.columns(c)
        rows = pl.ds(r * PATCHES, PATCHES)
        value = dot_nt(buf[rows, cols], wout[:, cols])
        if first:
            grad_att_ref[rows, :] = value
        else:
            grad_att_ref[rows, :] += value
        if r == 0:
            return
        shared = image_ref[:, cols].astype(bf16)
        value = dot_nn(att_turned_ref[...], buf[:, cols])
        value = value + dot_nn(hi, shared) + dot_nn(low, shared)
        grad_out[:, cols] = value.astype(bf16)
        store = pltpu.make_async_copy(
            grad_out.at[:, cols], grad_out_hbm.at[:, cols], out_sem.at[c]
        )
        store.start()
        stores.append(store)

    def side(i):
        if i < 2:
            keep_image(proj_own, pair_ref, kept, i)
        else:
            margin_piece(i - 2)

    gather.run(RETURN_STEPS, chunk, side, take_hop)

    def cotangent(i, rows, h):
        return grad_att_ref[rows, pl.ds(h * HS, HS)].astype(bf16)

    both_images(lambda i: back_image(kept, pair_ref, cotangent, own_grad_ref, i))
    scatter.finish()
    gather.finish()
    for copy in copies:
        copy.wait_send()
    for store in stores:
        store.wait()


def chain(rows, gain_row, gain_pair, pool_row, labels, qkv_local, out_local, head_local):
    return pl.pallas_call(
        chain_kernel,
        out_shape=(
            jax.ShapeDtypeStruct((ROWS, D), bf16),
            jax.ShapeDtypeStruct((D, TOTAL), bf16),
            jax.ShapeDtypeStruct((F, CLASSES), bf16),
            jax.ShapeDtypeStruct((1, 2), f32),
            jax.ShapeDtypeStruct((TOTAL, 3 * F), bf16),
            jax.ShapeDtypeStruct((F, D), bf16),
            jax.ShapeDtypeStruct((D, 3 * F), bf16),
        ),
        in_specs=[VM] * 5 + [ANY] * 3,
        out_specs=(VM, ANY, VM, VM, VM, ANY, ANY),
        scratch_shapes=[
            pltpu.VMEM((ROWS, D), bf16),
            pltpu.VMEM((F, TOTAL), bf16),
            pltpu.VMEM((TOTAL, 3 * F), bf16),
            pltpu.VMEM((8, D), f32),
            pltpu.VMEM((8, F), f32),
            pltpu.VMEM((D, 3 * F), bf16),
            pltpu.VMEM((F, D), bf16),
            pltpu.VMEM((D, CLASSES), bf16),
            pltpu.VMEM((TOTAL, D), bf16),
            pltpu.VMEM((TOTAL, D), bf16),
            pltpu.VMEM((TOTAL, D), bf16),
            pltpu.VMEM((TOTAL, 3 * F), f32),
            pltpu.VMEM((TOTAL, 3 * F), f32),
            pltpu.VMEM((D, TOTAL), bf16),
            pltpu.VMEM((D, TOTAL), bf16),
            pltpu.VMEM((TOTAL, F), bf16),
            pltpu.VMEM((TOTAL, D), bf16),
            pltpu.VMEM((7, ROWS, D), bf16),
            pltpu.VMEM((7, ROWS, D), bf16),
            pltpu.VMEM((ROWS, D), bf16),
            pltpu.VMEM((8, PACK), f32),
            pltpu.VMEM((len(PEERS), 8, PACK), f32),
            pltpu.VMEM((8, D), f32),
            pltpu.VMEM((8, D), f32),
            pltpu.VMEM((8, F), f32),
            pltpu.VMEM((ROWS, D), f32),
            pltpu.VMEM((ROWS, D), bf16),
            pltpu.VMEM((ROWS, D), bf16),
            pltpu.VMEM((F, D), bf16),
            pltpu.VMEM((TOTAL, F), f32),
            pltpu.SemaphoreType.DMA((5,)),
            pltpu.SemaphoreType.DMA((1,)),
            pltpu.SemaphoreType.DMA((len(OUT_PLAN),)),
            pltpu.SemaphoreType.DMA((len(OUT_PLAN),)),
            pltpu.SemaphoreType.DMA((len(PEERS),)),
            pltpu.SemaphoreType.DMA((len(PEERS),)),
            pltpu.SemaphoreType.DMA((len(RETURN_PLAN),)),
            pltpu.SemaphoreType.DMA((len(RETURN_PLAN),)),
            pltpu.SemaphoreType.DMA((len(RETURN_PLAN),)),
            pltpu.SemaphoreType.DMA((STEPS,)),
        ]
        + keep_scratch()
        + ring_sems(PROJECT_PLAN)
        + ring_sems(OUT_PLAN)
        + ring_sems(PROJECT_PLAN)
        + ring_sems(INPUT_PLAN)
        + ring_sems(RETURN_PLAN),
        compiler_params=params(0, 63 * 1024 * 1024),
        name="chain",
    )(rows, gain_row, gain_pair, pool_row, labels, qkv_local, out_local, head_local)


def finish_kernel(
    grad_ref,
    turned_hbm,
    part_hbm,
    out_in,
    grad_out_in,
    head_in,
    grad_hbm,
    out_hbm,
    grad_out_hbm,
    head_hbm,
    turned,
    part,
    result,
    passed_out,
    passed_grad,
    passed_head,
    load_sem,
    part_sem,
    store_sem,
    pass_sem,
):
    passes = [
        (out_in, passed_out, out_hbm),
        (grad_out_in, passed_grad, grad_out_hbm),
        (head_in, passed_head, head_hbm),
    ]
    def tall_rows(r):
        return pl.ds(pl.multiple_of(r * TALL, TALL), TALL)

    def load_pair(r):
        rows = tall_rows(r)
        return (
            pltpu.make_async_copy(turned_hbm.at[rows, :], turned.at[rows, :], load_sem.at[r]),
            pltpu.make_async_copy(part_hbm.at[rows, :], part.at[rows, :], part_sem.at[r]),
        )

    def store(r):
        rows = tall_rows(r)
        return pltpu.make_async_copy(
            result.at[:, rows, :], grad_hbm.at[:, rows, :], store_sem.at[r]
        )

    for r in range(STEPS):
        for load in load_pair(r):
            load.start()
    through = []
    for k, (source, held, _) in enumerate(passes):
        copy = pltpu.make_async_copy(source, held, pass_sem.at[k])
        copy.start()
        through.append(copy)

    def step(r, carry):
        rows = tall_rows(r)
        for load in load_pair(r):
            load.wait()
        value = dot_nn(turned[rows, :], grad_ref[...]) + part[rows, :].astype(f32)
        for t in range(3):
            result[t, rows, :] = value[:, t * F : (t + 1) * F].astype(bf16)
        store(r).start()
        return carry

    lax.fori_loop(0, STEPS // 2, step, 0)
    stores = []
    for k, (_, held, target) in enumerate(passes):
        through[k].wait()
        copy = pltpu.make_async_copy(held, target, pass_sem.at[k])
        copy.start()
        stores.append(copy)
    lax.fori_loop(STEPS // 2, STEPS, step, 0)
    for copy in stores:
        copy.wait()
    for r in range(STEPS):
        store(r).wait()


def finish(grad, turned, margin_part, out_own, grad_out, grad_head):
    return pl.pallas_call(
        finish_kernel,
        out_shape=(
            jax.ShapeDtypeStruct((3, D, F), bf16),
            jax.ShapeDtypeStruct((ROWS, D), bf16),
            jax.ShapeDtypeStruct((F, D), bf16),
            jax.ShapeDtypeStruct((F, CLASSES), bf16),
        ),
        in_specs=[VM] + [ANY] * 5,
        out_specs=(ANY,) * 4,
        scratch_shapes=[
            pltpu.VMEM((D, TOTAL), bf16),
            pltpu.VMEM((D, 3 * F), bf16),
            pltpu.VMEM((3, D, F), bf16),
            pltpu.VMEM((ROWS, D), bf16),
            pltpu.VMEM((F, D), bf16),
            pltpu.VMEM((F, CLASSES), bf16),
            pltpu.SemaphoreType.DMA((STEPS,)),
            pltpu.SemaphoreType.DMA((STEPS,)),
            pltpu.SemaphoreType.DMA((STEPS,)),
            pltpu.SemaphoreType.DMA((3,)),
        ],
        compiler_params=params(),
        name="finish",
    )(grad, turned, margin_part, out_own, grad_out, grad_head)


def on_device(
    block_inputs, qkv_weights, out_weights, norm_gain, query_key_gain, pool_gain, class_head, labels
):
    rows_in, qkv_local, out_local = block_inputs[0], qkv_weights[0], out_weights[0]
    gain_pair = query_key_gain[0]
    out_own, turned, grad_head, losses, own_grad, grad_out, margin_part = chain(
        rows_in, norm_gain, gain_pair, pool_gain, labels, qkv_local, out_local, class_head[0]
    )
    qkv_grad, out_own, grad_out, grad_head = finish(
        own_grad, turned, margin_part, out_own, grad_out, grad_head
    )
    return (out_own[None], qkv_grad[None], grad_out[None], grad_head[None], losses)


def solution(mesh):
    in_specs = (
        P("section", ("dp", "tensor"), None),
        P("section", None, None, ("dp", "tensor")),
        P("section", ("dp", "tensor"), None),
        P("section", None),
        P("section", None, None),
        P("section", None),
        P("section", None, None),
        P("section", None),
    )
    out_specs = (
        P("section", ("dp", "tensor"), None),
        P("section", None, None, ("dp", "tensor")),
        P("section", ("dp", "tensor"), None),
        P("section", ("dp", "tensor"), None),
        P("section", None),
    )
    return jax.shard_map(
        on_device, mesh=mesh, in_specs=in_specs, out_specs=out_specs, check_vma=False
    )
```
